32 devices in a mesh: gx: 8 (over z, y), gy: 4 (over x, core).
Axes of the slice: x: 2, y: 2, z: 4, core: 2. Of those that a mesh axis runs over, the one named last changes fastest.
Arguments:
- section_start: float32 [5, 64, 64, 512], P(None, None, 'gx', 'gy'), may hold values from -2 to 8, as said below
- section_now: float32 [5, 64, 64, 512], P(None, None, 'gx', 'gy'), may hold values from -2 to 8, as said below
- history: bfloat16 [255, 16, 64, 512], P(None, None, 'gx', 'gy'), may hold values from -9 to 9
Outputs:
- section_next: float32 [5, 64, 64, 512], P(None, None, 'gx', 'gy')
- triangle: float32 [256, 256], replicated
The draws below stay inside these ranges and needn't reach their ends.
Inputs may be any that keep to these rules, and one draw needn't show every extreme that they name: `section_start`: component 0 lies in [1, 2], components 1 to 3 are density times a velocity of magnitude at most 1 in each direction, and component 4 is at least the kinetic energy. `section_now`: as section_start.
All inputs are finite; a program needn't handle non-finite values.
Results may differ from the reference program's by a relative error of at most 0.0003.
Values sent between devices are 32-bit elements; how exact they have to be, the bound alone decides.
No kernel may reach another device: no remote copies, remote signals or barrier semaphores. Data moves between devices by JAX's collectives and lax.ppermute only.
A program may use at most 128 MiB of HBM per device.

```python
import math
import jax
import jax.numpy as jnp
from jax import lax

NZ = 64
CX = 8
SNAPS = 256
ZSUB = 4
NX = 64
NY = 512
N_GX = 8


def draw_state(key):
    key_list = jax.random.split(key, 3)
    grid_shape = (NZ, NX, NY)
    density = jax.random.uniform(key_list[0], grid_shape, jnp.float32, 1.0, 2.0)
    velocity = jnp.clip(0.5 * jax.random.normal(key_list[1], (3,) + grid_shape, jnp.float32), -1.0, 1.0)
    pressure = jax.random.uniform(key_list[2], grid_shape, jnp.float32, 0.5, 2.0)
    momentum = density[None] * velocity
    energy = pressure / 0.4 + 0.5 * density * (velocity[0] * velocity[0] + velocity[1] * velocity[1] + velocity[2] * velocity[2])
    return jnp.concatenate([density[None], momentum, energy[None]], axis=0)


def draw_section_start(key, part):
    return draw_state(jax.random.fold_in(key, 11))


def draw_section_now(key, part):
    return draw_state(jax.random.fold_in(key, 23))


def draw_history(key, part):
    key_list = jax.random.split(jax.random.fold_in(key, 37), 3)
    grid_shape = (NZ // ZSUB, NX, NY)
    scales = 0.2 * jnp.exp(jax.random.uniform(key_list[0], grid_shape, jnp.float32, 0.0, math.log(10.0)))
    common = jnp.clip(jax.random.normal(key_list[1], grid_shape, jnp.float32), -3.0, 3.0)
    noise = jnp.clip(jax.random.normal(key_list[2], (SNAPS - 1,) + grid_shape, jnp.float32), -3.0, 3.0)
    values = scales[None] * (0.5 * common[None] + noise)
    return values.astype(jnp.bfloat16)


def setup_inputs(seed: int = 0) -> dict:
    streams_of = jax.random.split(jax.random.key(seed), 4)
    section_start = draw_section_start(jax.random.fold_in(streams_of[3], 71), 0)
    section_now = draw_section_now(jax.random.fold_in(streams_of[3], 71), 0)
    history = draw_history(jax.random.fold_in(streams_of[3], 71), 0)
    return {"section_start": section_start, "section_now": section_now, "history": history}


GAMMA_LESS = 0.4
TIME_STEP = 0.2
VISCOUS = 0.25
BLOCK_PLANES = 8

def pressure_of(fields):
    kinetic = fields[1] * fields[1] + fields[2] * fields[2] + fields[3] * fields[3]
    return GAMMA_LESS * (fields[4] - 0.5 * kinetic / fields[0])

def flux_of(fields, direction):
    velocity = fields[direction] / fields[0]
    pressure = pressure_of(fields)
    columns = [fields[member] * velocity for member in range(4)]
    columns[direction] = columns[direction] + pressure
    columns.append((fields[4] + pressure) * velocity)
    return jnp.stack(columns, axis=0)

def tendency_block(padded):
    center = padded[:, 1:-1]
    flux_x = flux_of(center, 1)
    flux_y = flux_of(center, 2)
    flux_z = flux_of(padded, 3)
    divergence = 0.5 * (jnp.roll(flux_x, -1, 2) - jnp.roll(flux_x, 1, 2))
    divergence = divergence + 0.5 * (jnp.roll(flux_y, -1, 3) - jnp.roll(flux_y, 1, 3))
    divergence = divergence + 0.5 * (flux_z[:, 2:] - flux_z[:, :-2])
    laplacian = jnp.roll(center, -1, 2) + jnp.roll(center, 1, 2)
    laplacian = laplacian + jnp.roll(center, -1, 3) + jnp.roll(center, 1, 3)
    laplacian = laplacian + padded[:, 2:] + padded[:, :-2] - 6.0 * center
    return VISCOUS * laplacian - divergence

def reference(section_start, section_now, history):
    padded = jnp.concatenate([section_now[:, :1], section_now, section_now[:, -1:]], axis=1)
    block_count = NZ // BLOCK_PLANES

    def one_block(block_index):
        window = lax.dynamic_slice_in_dim(padded, block_index * BLOCK_PLANES, BLOCK_PLANES + 2, 1)
        return tendency_block(window)
    tendency = lax.map(one_block, jnp.arange(block_count, dtype=jnp.int32))
    tendency = jnp.moveaxis(tendency, 0, 1).reshape(5, NZ, NX, NY)
    section_next = 0.75 * section_start + 0.25 * (section_now + TIME_STEP * tendency)
    sample = section_next[:, ::ZSUB]
    snapshot = pressure_of(sample).astype(jnp.bfloat16)

    def add_block(running, block_index):
        older = lax.dynamic_slice_in_dim(history, block_index * CX, CX, 2).reshape(SNAPS - 1, -1)
        newest = lax.dynamic_slice_in_dim(snapshot, block_index * CX, CX, 1).reshape(1, -1)
        matrix = jnp.concatenate([older, newest], axis=0)
        product = lax.dot_general(matrix.astype(jnp.float32), matrix.astype(jnp.float32), (((1,), (1,)), ((), ())), preferred_element_type=jnp.float32)
        return (running + product, None)
    gram_total, _ = lax.scan(add_block, jnp.zeros((SNAPS, SNAPS), jnp.float32), jnp.arange(N_GX, dtype=jnp.int32))
    rows_total = NZ // ZSUB * NX * NY
    triangle = jnp.linalg.cholesky(gram_total / rows_total).T
    return (section_next, triangle)
```

```python
import jax
import jax.numpy as jnp
from jax import lax
from jax.experimental import pallas as pl
from jax.experimental.pallas import tpu as pltpu
from jax.sharding import PartitionSpec as P

ZSUB = 4
GAMMA_LESS = 0.4
TIME_STEP = 0.2
VISCOUS = 0.25
CHUNK = 8


def iota(shape, dim):
    return lax.broadcasted_iota(jnp.int32, shape, dim)


def edges_body(now_ref, cols_ref, lo_ref, hi_ref):
    planes, rows, lanes = now_ref.shape
    key = lax.rem((iota((rows, lanes), 1) + 1) // 2, planes)
    packed = jnp.zeros((rows, lanes), jnp.float32)
    for z in range(planes):
        cells = now_ref[z]
        rolled = pltpu.roll(cells, 2 * z, 1) if z else cells
        packed = jnp.where(key == z, rolled, packed)
    cols_ref[...] = packed
    lo_ref[...] = now_ref[:, 0, :]
    hi_ref[...] = now_ref[:, rows - 1, :]


def edges(now):
    fields, planes, rows, lanes = now.shape
    assert 2 * planes == lanes
    row_spec = pl.BlockSpec((None, planes, lanes), lambda f: (f, 0, 0))
    return pl.pallas_call(
        edges_body,
        out_shape=(
            jax.ShapeDtypeStruct((fields, rows, lanes), now.dtype),
            jax.ShapeDtypeStruct((fields, planes, lanes), now.dtype),
            jax.ShapeDtypeStruct((fields, planes, lanes), now.dtype),
        ),
        grid=(fields,),
        in_specs=[pl.BlockSpec((None, planes, rows, lanes), lambda f: (f, 0, 0, 0))],
        out_specs=(pl.BlockSpec((None, rows, lanes), lambda f: (f, 0, 0)), row_spec, row_spec),
        name="edges",
    )(now)


def state_of(q):
    inverse = 1.0 / q[0]
    speed = [q[k] * inverse for k in (1, 2, 3)]
    kinetic = q[1] * speed[0] + q[2] * speed[1] + q[3] * speed[2]
    pressure = GAMMA_LESS * (q[4] - 0.5 * kinetic)
    return speed, pressure


def flux_of(q, state, direction):
    speed, pressure = state
    u = speed[direction - 1]
    columns = [q[direction]] + [q[k] * u for k in (1, 2, 3)] + [(q[4] + pressure) * u]
    columns[direction] = columns[direction] + pressure
    return columns


def ahead_of(q, flux):
    return [VISCOUS * a - 0.5 * b for a, b in zip(q, flux)]


def behind_of(q, flux):
    return [VISCOUS * a + 0.5 * b for a, b in zip(q, flux)]


def stencil_body(now_ref, start_ref, left_ref, right_ref, xlo_ref, xhi_ref, next_ref, press_ref, halo_ref):
    fields, planes, rows, lanes = now_ref.shape
    chunk = start_ref.shape[1]
    step = pl.program_id(0)
    base = step * chunk
    lane = iota((rows, lanes), 1)
    row = iota((rows, lanes), 0)
    span = range(fields)

    @pl.when(step == 0)
    def _():
        right = [right_ref[f] for f in span]
        left = [left_ref[f] for f in span]
        ahead = ahead_of(right, flux_of(right, state_of(right), 2))
        behind = behind_of(left, flux_of(left, state_of(left), 2))
        for f in span:
            halo_ref[f] = jnp.where(lane % 2 == 0, ahead[f], pltpu.roll(behind[f], 2, 1))

    def z_parts(z):
        q = [now_ref[f, z] for f in span]
        flux = flux_of(q, state_of(q), 3)
        return ahead_of(q, flux), behind_of(q, flux)

    lo = [xlo_ref[f] for f in span]
    hi = [xhi_ref[f] for f in span]
    x_behind = behind_of(lo, flux_of(lo, state_of(lo), 1))
    x_ahead = ahead_of(hi, flux_of(hi, state_of(hi), 1))
    turn = lax.rem(lanes - 2 * base, lanes)
    halo = [pltpu.roll(halo_ref[f], turn, 1) for f in span]

    _, before = z_parts(jnp.maximum(base - 1, 0))
    pending = None

    def finish(j, tendency):
        out = []
        for f in span:
            value = 0.75 * start_ref[f, j] + 0.25 * (now_ref[f, base + j] + TIME_STEP * tendency[f])
            next_ref[f, j] = value
            out.append(value)
        if j % ZSUB == 0:
            press_ref[j // ZSUB] = state_of(out)[1]

    for j in range(chunk):
        q = [now_ref[f, base + j] for f in span]
        state = state_of(q)
        flux = flux_of(q, state, 3)
        ahead, behind = ahead_of(q, flux), behind_of(q, flux)
        if pending is not None:
            finish(j - 1, [pending[f] + ahead[f] for f in span])
        flux_y = flux_of(q, state, 2)
        flux_x = flux_of(q, state, 1)
        y_ahead, y_behind = ahead_of(q, flux_y), behind_of(q, flux_y)
        a_x, b_x = ahead_of(q, flux_x), behind_of(q, flux_x)
        pending = []
        for f in span:
            edge = pltpu.roll(halo[f], lanes - 1 - 2 * j, 1)
            y_part = jnp.where(lane == lanes - 1, edge, pltpu.roll(y_ahead[f], lanes - 1, 1))
            y_part = y_part + jnp.where(lane == 0, edge, pltpu.roll(y_behind[f], 1, 1))
            x_part = jnp.where(row == rows - 1, x_ahead[f][j : j + 1], pltpu.roll(a_x[f], rows - 1, 0))
            x_part = x_part + jnp.where(row == 0, x_behind[f][j : j + 1], pltpu.roll(b_x[f], 1, 0))
            pending.append((x_part + y_part) + (before[f] - 6.0 * VISCOUS * q[f]))
        before = behind
    ahead, _ = z_parts(jnp.minimum(base + chunk, planes - 1))
    finish(chunk - 1, [pending[f] + ahead[f] for f in span])


def stencil(now, start, left, right, xlo, xhi):
    fields, planes, rows, lanes = now.shape
    chunk = CHUNK
    whole = pl.BlockSpec((fields, rows, lanes), lambda c: (0, 0, 0))
    part = pl.BlockSpec((fields, chunk, rows, lanes), lambda c: (0, c, 0, 0))
    line = pl.BlockSpec((fields, chunk, lanes), lambda c: (0, c, 0))
    return pl.pallas_call(
        stencil_body,
        out_shape=(
            jax.ShapeDtypeStruct(now.shape, now.dtype),
            jax.ShapeDtypeStruct((planes // ZSUB, rows, lanes), now.dtype),
        ),
        grid=(planes // chunk,),
        in_specs=[
            pl.BlockSpec((fields, planes, rows, lanes), lambda c: (0, 0, 0, 0)),
            part, whole, whole, line, line,
        ],
        out_specs=(part, pl.BlockSpec((chunk // ZSUB, rows, lanes), lambda c: (c, 0, 0))),
        scratch_shapes=[pltpu.VMEM((fields, rows, lanes), jnp.float32)],
        name="stencil",
    )(now, start, left, right, xlo, xhi)


def gram_body(older_ref, newest_ref, out_ref, cells_ref, total_ref):
    older, rows, lanes = older_ref.shape
    snaps = total_ref.shape[0]
    step = pl.program_id(0)

    @pl.when(step == 0)
    def _():
        total_ref[...] = jnp.zeros_like(total_ref)

    cells_ref[pl.ds(0, older * rows), :] = older_ref[...].astype(jnp.float32).reshape(older * rows, lanes)
    cells_ref[pl.ds(older * rows, rows), :] = newest_ref[...]
    parts = [cells_ref[pl.ds(r, snaps, stride=rows), :].astype(jnp.bfloat16) for r in range(rows)]
    matrix = jnp.concatenate(parts, axis=1)
    total_ref[...] += lax.dot_general(
        matrix, matrix, (((1,), (1,)), ((), ())), preferred_element_type=jnp.float32
    )

    @pl.when(step == pl.num_programs(0) - 1)
    def _():
        half = snaps // 2
        first = total_ref[:half, :half]
        last = total_ref[half:, half:]
        r, c = iota((half, half), 0), iota((half, half), 1)
        out_ref[:half] = jnp.where(r <= c, first, last)
        out_ref[half : 2 * half] = total_ref[:half, half:]
        diagonal = jnp.sum(jnp.where(r == c, last, 0.0), axis=0, keepdims=True)
        out_ref[2 * half :] = jnp.broadcast_to(diagonal, (out_ref.shape[0] - 2 * half, half))


def gram(history, newest):
    older, planes, rows, lanes = history.shape
    snaps = older + 1
    half = snaps // 2
    return pl.pallas_call(
        gram_body,
        out_shape=jax.ShapeDtypeStruct((2 * half + 16, half), jnp.float32),
        grid=(planes,),
        in_specs=[
            pl.BlockSpec((older, None, rows, lanes), lambda p: (0, p, 0, 0)),
            pl.BlockSpec((None, rows, lanes), lambda p: (p, 0, 0)),
        ],
        out_specs=pl.BlockSpec((2 * half + 16, half), lambda p: (0, 0)),
        scratch_shapes=[
            pltpu.VMEM((snaps * rows, lanes), jnp.float32),
            pltpu.VMEM((snaps, snaps), jnp.float32),
        ],
        name="gram",
    )(history, newest)


def unfold(folded):
    half = folded.shape[1]
    mixed, cross = folded[:half], folded[half : 2 * half]
    r, c = iota((half, half), 0), iota((half, half), 1)
    first = jnp.where(r <= c, mixed, mixed.T)
    last = jnp.where(r == c, folded[2 * half][None], jnp.where(r > c, mixed, mixed.T))
    return jnp.block([[first, cross], [cross.T, last]])


def total_over(values, axes):
    count = 1
    for axis in axes:
        count *= lax.axis_size(axis)
    here = lax.axis_index(axes)

    def swap(part, bit):
        return lax.ppermute(part, axes, [(i, i ^ bit) for i in range(count)])

    size = values.shape[0] // 2
    side = here % 2
    halves = values.reshape(2, size, -1)
    mine = lax.dynamic_index_in_dim(halves, side, 0, False)
    sent = lax.dynamic_index_in_dim(halves, 1 - side, 0, False)
    mine = mine + swap(sent, 1)
    bit = 2
    while bit < count:
        mine = mine + swap(mine, bit)
        bit *= 2
    other = swap(mine, 1)
    first = jnp.where(side == 0, mine, other)
    second = jnp.where(side == 0, other, mine)
    return jnp.concatenate([first, second])


def local(section_start, section_now, history):
    cols, lo, hi = edges(section_now)

    def shifted(part, axis, by):
        count = lax.axis_size(axis)
        return lax.ppermute(part, axis, [(i, (i + by) % count) for i in range(count)])

    left, right = shifted(cols, "gy", 1), shifted(cols, "gy", -1)
    xlo, xhi = shifted(hi, "gx", 1), shifted(lo, "gx", -1)
    section_next, newest = stencil(section_now, section_start, left, right, xlo, xhi)
    folded = gram(history, newest)
    rows_total = newest.size * lax.axis_size("gx") * lax.axis_size("gy")
    gram_total = unfold(total_over(folded, ("gx", "gy")) / rows_total)
    triangle = lax.linalg.cholesky(gram_total, symmetrize_input=False).T
    return (section_next, triangle)


def solution(mesh):
    placed = P(None, None, "gx", "gy")
    return jax.shard_map(
        local,
        mesh=mesh,
        in_specs=(placed, placed, placed),
        out_specs=(placed, P()),
        check_vma=False,
    )
```

```python
import functools

import jax
import jax.numpy as jnp
from jax import lax
from jax.experimental import pallas as pl
from jax.experimental.pallas import tpu as pltpu
from jax.sharding import PartitionSpec as P

ZSUB = 4
GAMMA_LESS = 0.4
TIME_STEP = 0.2
VISCOUS = 0.25
CHUNK = 8


def iota(shape, dim):
    return lax.broadcasted_iota(jnp.int32, shape, dim)


def edges_body(now_ref, cols_ref, lo_ref, hi_ref):
    planes, rows, lanes = now_ref.shape
    key = lax.rem((iota((rows, lanes), 1) + 1) // 2, planes)
    packed = jnp.zeros((rows, lanes), jnp.float32)
    for z in range(planes):
        cells = now_ref[z]
        rolled = pltpu.roll(cells, 2 * z, 1) if z else cells
        packed = jnp.where(key == z, rolled, packed)
    cols_ref[...] = packed
    lo_ref[...] = now_ref[:, 0, :]
    hi_ref[...] = now_ref[:, rows - 1, :]


def edges(now):
    fields, planes, rows, lanes = now.shape
    assert 2 * planes == lanes
    row_spec = pl.BlockSpec((None, planes, lanes), lambda f: (f, 0, 0))
    return pl.pallas_call(
        edges_body,
        out_shape=(
            jax.ShapeDtypeStruct((fields, rows, lanes), now.dtype),
            jax.ShapeDtypeStruct((fields, planes, lanes), now.dtype),
            jax.ShapeDtypeStruct((fields, planes, lanes), now.dtype),
        ),
        grid=(fields,),
        in_specs=[pl.BlockSpec((None, planes, rows, lanes), lambda f: (f, 0, 0, 0))],
        out_specs=(pl.BlockSpec((None, rows, lanes), lambda f: (f, 0, 0)), row_spec, row_spec),
        name="edges",
    )(now)


def state_of(q):
    inverse = 1.0 / q[0]
    speed = [q[k] * inverse for k in (1, 2, 3)]
    kinetic = q[1] * speed[0] + q[2] * speed[1] + q[3] * speed[2]
    pressure = GAMMA_LESS * (q[4] - 0.5 * kinetic)
    return speed, pressure


def flux_of(q, state, direction):
    speed, pressure = state
    u = speed[direction - 1]
    columns = [q[direction]] + [q[k] * u for k in (1, 2, 3)] + [(q[4] + pressure) * u]
    columns[direction] = columns[direction] + pressure
    return columns


def ahead_of(q, flux):
    return [VISCOUS * a - 0.5 * b for a, b in zip(q, flux)]


def behind_of(q, flux):
    return [VISCOUS * a + 0.5 * b for a, b in zip(q, flux)]


def stencil_body(now_ref, start_ref, left_ref, right_ref, xlo_ref, xhi_ref, next_ref, press_ref, halo_ref):
    fields, planes, rows, lanes = now_ref.shape
    chunk = start_ref.shape[1]
    step = pl.program_id(0)
    base = step * chunk
    lane = iota((rows, lanes), 1)
    row = iota((rows, lanes), 0)
    span = range(fields)

    @pl.when(step == 0)
    def _():
        right = [right_ref[f] for f in span]
        left = [left_ref[f] for f in span]
        ahead = ahead_of(right, flux_of(right, state_of(right), 2))
        behind = behind_of(left, flux_of(left, state_of(left), 2))
        for f in span:
            halo_ref[f] = jnp.where(lane % 2 == 0, ahead[f], pltpu.roll(behind[f], 2, 1))

    def z_parts(z):
        q = [now_ref[f, z] for f in span]
        flux = flux_of(q, state_of(q), 3)
        return ahead_of(q, flux), behind_of(q, flux)

    lo = [xlo_ref[f] for f in span]
    hi = [xhi_ref[f] for f in span]
    x_behind = behind_of(lo, flux_of(lo, state_of(lo), 1))
    x_ahead = ahead_of(hi, flux_of(hi, state_of(hi), 1))
    turn = lax.rem(lanes - 2 * base, lanes)
    halo = [pltpu.roll(halo_ref[f], turn, 1) for f in span]

    _, before = z_parts(jnp.maximum(base - 1, 0))
    pending = None

    def finish(j, tendency):
        out = []
        for f in span:
            value = 0.75 * start_ref[f, j] + 0.25 * (now_ref[f, base + j] + TIME_STEP * tendency[f])
            next_ref[f, j] = value
            out.append(value)
        if j % ZSUB == 0:
            press_ref[j // ZSUB] = state_of(out)[1]

    for j in range(chunk):
        q = [now_ref[f, base + j] for f in span]
        state = state_of(q)
        flux = flux_of(q, state, 3)
        ahead, behind = ahead_of(q, flux), behind_of(q, flux)
        if pending is not None:
            finish(j - 1, [pending[f] + ahead[f] for f in span])
        flux_y = flux_of(q, state, 2)
        flux_x = flux_of(q, state, 1)
        y_ahead, y_behind = ahead_of(q, flux_y), behind_of(q, flux_y)
        a_x, b_x = ahead_of(q, flux_x), behind_of(q, flux_x)
        pending = []
        for f in span:
            edge = pltpu.roll(halo[f], lanes - 1 - 2 * j, 1)
            y_part = jnp.where(lane == lanes - 1, edge, pltpu.roll(y_ahead[f], lanes - 1, 1))
            y_part = y_part + jnp.where(lane == 0, edge, pltpu.roll(y_behind[f], 1, 1))
            x_part = jnp.where(row == rows - 1, x_ahead[f][j : j + 1], pltpu.roll(a_x[f], rows - 1, 0))
            x_part = x_part + jnp.where(row == 0, x_behind[f][j : j + 1], pltpu.roll(b_x[f], 1, 0))
            pending.append((x_part + y_part) + (before[f] - 6.0 * VISCOUS * q[f]))
        before = behind
    ahead, _ = z_parts(jnp.minimum(base + chunk, planes - 1))
    finish(chunk - 1, [pending[f] + ahead[f] for f in span])


def stencil(now, start, left, right, xlo, xhi):
    fields, planes, rows, lanes = now.shape
    chunk = CHUNK
    whole = pl.BlockSpec((fields, rows, lanes), lambda c: (0, 0, 0))
    part = pl.BlockSpec((fields, chunk, rows, lanes), lambda c: (0, c, 0, 0))
    line = pl.BlockSpec((fields, chunk, lanes), lambda c: (0, c, 0))
    return pl.pallas_call(
        stencil_body,
        out_shape=(
            jax.ShapeDtypeStruct(now.shape, now.dtype),
            jax.ShapeDtypeStruct((planes // ZSUB, rows, lanes), now.dtype),
        ),
        grid=(planes // chunk,),
        in_specs=[
            pl.BlockSpec((fields, planes, rows, lanes), lambda c: (0, 0, 0, 0)),
            part, whole, whole, line, line,
        ],
        out_specs=(part, pl.BlockSpec((chunk // ZSUB, rows, lanes), lambda c: (c, 0, 0))),
        scratch_shapes=[pltpu.VMEM((fields, rows, lanes), jnp.float32)],
        name="stencil",
    )(now, start, left, right, xlo, xhi)


def gram_body(older_ref, newest_ref, out_ref, cells_ref, total_ref):
    older, rows, lanes = older_ref.shape
    snaps = total_ref.shape[0]
    step = pl.program_id(0)

    @pl.when(step == 0)
    def _():
        total_ref[...] = jnp.zeros_like(total_ref)

    cells_ref[pl.ds(0, older * rows), :] = older_ref[...].astype(jnp.float32).reshape(older * rows, lanes)
    cells_ref[pl.ds(older * rows, rows), :] = newest_ref[...]
    parts = [cells_ref[pl.ds(r, snaps, stride=rows), :].astype(jnp.bfloat16) for r in range(rows)]
    matrix = jnp.concatenate(parts, axis=1)
    total_ref[...] += lax.dot_general(
        matrix, matrix, (((1,), (1,)), ((), ())), preferred_element_type=jnp.float32
    )

    @pl.when(step == pl.num_programs(0) - 1)
    def _():
        half = snaps // 2
        first = total_ref[:half, :half]
        last = total_ref[half:, half:]
        r, c = iota((half, half), 0), iota((half, half), 1)
        out_ref[:half] = jnp.where(r <= c, first, last)
        out_ref[half : 2 * half] = total_ref[:half, half:]
        diagonal = jnp.sum(jnp.where(r == c, last, 0.0), axis=0, keepdims=True)
        out_ref[2 * half :] = jnp.broadcast_to(diagonal, (out_ref.shape[0] - 2 * half, half))


def gram(history, newest):
    older, planes, rows, lanes = history.shape
    snaps = older + 1
    half = snaps // 2
    return pl.pallas_call(
        gram_body,
        out_shape=jax.ShapeDtypeStruct((2 * half + 16, half), jnp.float32),
        grid=(planes,),
        in_specs=[
            pl.BlockSpec((older, None, rows, lanes), lambda p: (0, p, 0, 0)),
            pl.BlockSpec((None, rows, lanes), lambda p: (p, 0, 0)),
        ],
        out_specs=pl.BlockSpec((2 * half + 16, half), lambda p: (0, 0)),
        scratch_shapes=[
            pltpu.VMEM((snaps * rows, lanes), jnp.float32),
            pltpu.VMEM((snaps, snaps), jnp.float32),
        ],
        name="gram",
    )(history, newest)


def factor_body(scale, folded_ref, out_ref, gram_ref):
    half = folded_ref.shape[1]
    group = 8
    r, c = iota((half, half), 0), iota((half, half), 1)
    mixed = folded_ref[:half] * scale
    turned = mixed.T
    gram_ref[:half, :half] = jnp.where(r <= c, mixed, turned)
    gram_ref[:half, half:] = folded_ref[half : 2 * half] * scale
    diagonal = jnp.broadcast_to(folded_ref[2 * half : 2 * half + 1] * scale, (half, half))
    gram_ref[half:, half:] = jnp.where(r == c, diagonal, jnp.where(r > c, mixed, turned))
    out_ref[half:, :half] = jnp.zeros((half, half), jnp.float32)
    sub, lane = iota((group, half), 0), iota((group, half), 1)
    span = range(group)

    def column(x, index):
        return jnp.broadcast_to(x[:, index : index + 1], (group, half))

    def line(x, index):
        return jnp.broadcast_to(x[index : index + 1, :], (group, half))

    per = half // group
    for panel in range(2):
        width = 2 - panel
        tiles = [
            [
                gram_ref[pl.ds(panel * half + group * t, group), pl.ds((panel + v) * half, half)]
                for v in range(width)
            ]
            for t in range(per)
        ]
        for t in range(per):
            first = group * t
            own = [column(tiles[t][0], first + j) for j in span]
            pivot = {(i, j): line(own[j], i) for j in span for i in range(j + 1)}
            rows = [[line(x, i) for x in tiles[t]] for i in span]
            later = range(t + 1, per)
            lower = {m: [column(tiles[m][0], first + j) for j in span] for m in later}
            for i in span:
                inverse = lax.rsqrt(pivot[i, i])
                for j in range(i + 1, group):
                    pivot[i, j] = pivot[i, j] * inverse
                for j in range(i + 1, group):
                    for k in range(j, group):
                        pivot[j, k] = pivot[j, k] - pivot[i, j] * pivot[i, k]
                rows[i] = [x * inverse for x in rows[i]]
                for j in range(i + 1, group):
                    rows[j] = [a - pivot[i, j] * b for a, b in zip(rows[j], rows[i])]
                for m in later:
                    entry = lower[m][i] * inverse
                    for j in range(i + 1, group):
                        lower[m][j] = lower[m][j] - entry * pivot[i, j]
                    tiles[m] = [a - entry * b for a, b in zip(tiles[m], rows[i])]
            for v in range(width):
                merged = rows[0][v]
                for i in range(1, group):
                    merged = jnp.where(sub == i, rows[i][v], merged)
                if v == 0:
                    merged = jnp.where(lane >= first + sub, merged, 0.0)
                out_ref[pl.ds(panel * half + first, group), pl.ds((panel + v) * half, half)] = merged
        if panel == 0:
            across = out_ref[:half, half:]
            gram_ref[half:, half:] = gram_ref[half:, half:] - lax.dot_general(
                across,
                across,
                (((0,), (0,)), ((), ())),
                precision=lax.Precision.HIGHEST,
                preferred_element_type=jnp.float32,
            )


def factor(folded, rows_total):
    snaps = 2 * folded.shape[1]
    return pl.pallas_call(
        functools.partial(factor_body, 1.0 / rows_total),
        out_shape=jax.ShapeDtypeStruct((snaps, snaps), jnp.float32),
        in_specs=[pl.BlockSpec(memory_space=pltpu.VMEM)],
        out_specs=pl.BlockSpec(memory_space=pltpu.VMEM),
        scratch_shapes=[pltpu.VMEM((snaps, snaps), jnp.float32)],
        name="factor",
    )(folded)


def total_over(values, axes):
    count = 1
    for axis in axes:
        count *= lax.axis_size(axis)
    here = lax.axis_index(axes)

    def swap(part, bit):
        return lax.ppermute(part, axes, [(i, i ^ bit) for i in range(count)])

    size = values.shape[0] // 2
    side = here % 2
    halves = values.reshape(2, size, -1)
    mine = lax.dynamic_index_in_dim(halves, side, 0, False)
    sent = lax.dynamic_index_in_dim(halves, 1 - side, 0, False)
    mine = mine + swap(sent, 1)
    bit = 2
    while bit < count:
        mine = mine + swap(mine, bit)
        bit *= 2
    other = swap(mine, 1)
    first = jnp.where(side == 0, mine, other)
    second = jnp.where(side == 0, other, mine)
    return jnp.concatenate([first, second])


def local(section_start, section_now, history):
    cols, lo, hi = edges(section_now)

    def shifted(part, axis, by):
        count = lax.axis_size(axis)
        return lax.ppermute(part, axis, [(i, (i + by) % count) for i in range(count)])

    left, right = shifted(cols, "gy", 1), shifted(cols, "gy", -1)
    xlo, xhi = shifted(hi, "gx", 1), shifted(lo, "gx", -1)
    section_next, newest = stencil(section_now, section_start, left, right, xlo, xhi)
    folded = gram(history, newest)
    rows_total = newest.size * lax.axis_size("gx") * lax.axis_size("gy")
    triangle = factor(total_over(folded, ("gx", "gy")), rows_total)
    return (section_next, triangle)


def solution(mesh):
    placed = P(None, None, "gx", "gy")
    return jax.shard_map(
        local,
        mesh=mesh,
        in_specs=(placed, placed, placed),
        out_specs=(placed, P()),
        check_vma=False,
    )
```

```python
import functools

import jax
import jax.numpy as jnp
from jax import lax
from jax.experimental import pallas as pl
from jax.experimental.pallas import tpu as pltpu
from jax.sharding import PartitionSpec as P

ZSUB = 4
GAMMA_LESS = 0.4
TIME_STEP = 0.2
VISCOUS = 0.25
CHUNK = 8


def iota(shape, dim):
    return lax.broadcasted_iota(jnp.int32, shape, dim)


def edges_body(now_ref, lo_ref, hi_ref, cols_ref):
    fields, planes, rows, lanes = now_ref.shape
    lo_ref[...] = now_ref[:, :, 0, :]
    hi_ref[...] = now_ref[:, :, rows - 1, :]
    key = lax.rem((iota((rows, lanes), 1) + 1) // 2, planes)
    masks = 8
    for f in range(fields):
        parts = [jnp.zeros((rows, lanes), jnp.float32)] * masks
        for z in range(planes):
            cells = now_ref[f, z]
            rolled = pltpu.roll(cells, 2 * z, 1) if z else cells
            parts[z % masks] = jnp.where(key == z, rolled, parts[z % masks])
        while len(parts) > 1:
            parts = [x + y for x, y in zip(parts[::2], parts[1::2])]
        cols_ref[f] = parts[0]


def edges(now):
    fields, planes, rows, lanes = now.shape
    assert 2 * planes == lanes
    line = jax.ShapeDtypeStruct((fields, planes, lanes), now.dtype)
    in_vmem = pl.BlockSpec(memory_space=pltpu.VMEM)
    return pl.pallas_call(
        edges_body,
        out_shape=(line, line, jax.ShapeDtypeStruct((fields, rows, lanes), now.dtype)),
        in_specs=[in_vmem],
        out_specs=(in_vmem, in_vmem, in_vmem),
        name="edges",
    )(now)


def state_of(q):
    inverse = 1.0 / q[0]
    speed = [q[k] * inverse for k in (1, 2, 3)]
    twice = q[1] * speed[0] + q[2] * speed[1] + q[3] * speed[2]
    return speed, GAMMA_LESS * (q[4] - 0.5 * twice)


def products_of(q, state):
    speed, pressure = state
    total = q[4] + pressure
    shared = {}
    for i in range(3):
        for j in range(i, 3):
            shared[i, j] = q[1 + i] * speed[j]
    return shared, total


def flux_of(q, state, direction, products=None):
    speed, pressure = state
    shared, total = products or products_of(q, state)
    d = direction - 1
    columns = [q[direction]] + [shared[min(i, d), max(i, d)] for i in range(3)] + [total * speed[d]]
    columns[direction] = columns[direction] + pressure
    return columns


def scaled(q):
    return [2.0 * VISCOUS * x for x in q]


def ahead_of(base, flux):
    return [a - b for a, b in zip(base, flux)]


def behind_of(base, flux):
    return [a + b for a, b in zip(base, flux)]


def only_ahead(q, direction):
    return ahead_of(scaled(q), flux_of(q, state_of(q), direction))


def only_behind(q, direction):
    return behind_of(scaled(q), flux_of(q, state_of(q), direction))


def y_halo(left, right):
    ahead, behind = only_ahead(right, 2), only_behind(left, 2)
    even = iota(ahead[0].shape, 1) % 2 == 0
    return [jnp.where(even, a, pltpu.roll(b, 2, 1)) for a, b in zip(ahead, behind)]


def within_plane(q, base, state, products, edge, x_ahead, x_behind):
    rows, lanes = q[0].shape
    row, lane = iota((rows, lanes), 0), iota((rows, lanes), 1)
    y = flux_of(q, state, 2, products)
    x = flux_of(q, state, 1, products)
    y_a, y_b, x_a, x_b = ahead_of(base, y), behind_of(base, y), ahead_of(base, x), behind_of(base, x)
    sums = []
    for f in range(len(q)):
        part = jnp.where(lane == lanes - 1, edge[f], pltpu.roll(y_a[f], lanes - 1, 1))
        part = part + jnp.where(lane == 0, edge[f], pltpu.roll(y_b[f], 1, 1))
        other = jnp.where(row == rows - 1, x_ahead[f], pltpu.roll(x_a[f], rows - 1, 0))
        other = other + jnp.where(row == 0, x_behind[f], pltpu.roll(x_b[f], 1, 0))
        sums.append(part + other)
    return sums


def advanced(start, now, total):
    return 0.75 * start + (0.25 * (1.0 - 6.0 * VISCOUS * TIME_STEP)) * now + (0.125 * TIME_STEP) * total


def stencil_body(first, *refs):
    now_ref, start_ref, left_ref, right_ref, xlo_ref, xhi_ref = refs[:6]
    next_ref, halo_ref = refs[-2:]
    fields, planes, rows, lanes = now_ref.shape
    chunk = start_ref.shape[1]
    step = pl.program_id(0)
    base = (first + step) * chunk
    span = range(fields)

    @pl.when(step == 0)
    def _():
        packed = y_halo([left_ref[f] for f in span], [right_ref[f] for f in span])
        for f in span:
            halo_ref[f] = packed[f]

    x_behind = only_behind([xlo_ref[f] for f in span], 1)
    x_ahead = only_ahead([xhi_ref[f] for f in span], 1)
    turn = lax.rem(lanes - 2 * base, lanes)
    halo = [pltpu.roll(halo_ref[f], turn, 1) for f in span]
    z = jnp.maximum(base - 1, 0)
    before = only_behind([now_ref[f, z] for f in span], 3)
    pending = None

    def finish(j, ahead):
        for f in span:
            next_ref[f, j] = advanced(start_ref[f, j], now_ref[f, base + j], pending[f] + ahead[f])

    for j in range(chunk):
        q = [now_ref[f, base + j] for f in span]
        state = state_of(q)
        products = products_of(q, state)
        half = scaled(q)
        flux = flux_of(q, state, 3, products)
        if pending is not None:
            finish(j - 1, ahead_of(half, flux))
        edge = [pltpu.roll(halo[f], lanes - 1 - 2 * j, 1) for f in span]
        sums = within_plane(
            q, half, state, products, edge,
            [x_ahead[f][j : j + 1] for f in span], [x_behind[f][j : j + 1] for f in span],
        )
        pending = [sums[f] + before[f] for f in span]
        before = behind_of(half, flux)
    z = jnp.minimum(base + chunk, planes - 1)
    finish(chunk - 1, only_ahead([now_ref[f, z] for f in span], 3))


def stencil(now, start, left, right, xlo, xhi, first, count, into):
    fields, planes, rows, lanes = now.shape
    chunk = CHUNK
    whole = pl.BlockSpec((fields, rows, lanes), lambda c: (0, 0, 0))
    part = pl.BlockSpec((fields, chunk, rows, lanes), lambda c: (0, first + c, 0, 0))
    line = pl.BlockSpec((fields, chunk, lanes), lambda c: (0, first + c, 0))
    specs = [
        pl.BlockSpec((fields, planes, rows, lanes), lambda c: (0, 0, 0, 0)),
        part, whole, whole, line, line,
    ]
    operands = [now, start, left, right, xlo, xhi]
    if into is not None:
        specs.append(pl.BlockSpec(memory_space=pl.ANY))
        operands.append(into)
    return pl.pallas_call(
        functools.partial(stencil_body, first),
        out_shape=jax.ShapeDtypeStruct(now.shape, now.dtype),
        grid=(count,),
        in_specs=specs,
        out_specs=part,
        scratch_shapes=[pltpu.VMEM((fields, rows, lanes), jnp.float32)],
        input_output_aliases={} if into is None else {len(operands) - 1: 0},
        name=f"stencil_{first}",
    )(*operands)


def gram_body(
    older_ref, below_ref, now_ref, above_ref, start_ref, left_ref, right_ref, xlo_ref, xhi_ref,
    mine_ref, sent_ref, even_ref, odd_ref, total_ref, halo_ref, folded_ref, *, axis,
):
    older, pair, rows, lanes = older_ref.shape
    fields = halo_ref.shape[0]
    snaps = total_ref.shape[0]
    step = pl.program_id(0)
    span = range(fields)

    @pl.when(step == 0)
    def _():
        total_ref[...] = jnp.zeros_like(total_ref)
        odd_ref[...] = jnp.zeros_like(odd_ref)
        packed = y_halo([left_ref[f] for f in span], [right_ref[f] for f in span])
        for f in span:
            halo_ref[f] = packed[f]

    def parts_of(ref):
        return [ref[pl.ds(r, snaps, stride=rows), :].astype(jnp.bfloat16) for r in range(rows)]

    def newest(which):
        z = ZSUB * (pair * step + which)
        q = [now_ref[f, which, 0] for f in span]
        state = state_of(q)
        products = products_of(q, state)
        half = scaled(q)
        turn = lax.rem(2 * lanes - 1 - 2 * z, lanes)
        edge = [pltpu.roll(halo_ref[f], turn, 1) for f in span]
        x_behind = only_behind([xlo_ref[f, pl.ds(z, 1), :] for f in span], 1)
        x_ahead = only_ahead([xhi_ref[f, pl.ds(z, 1), :] for f in span], 1)
        sums = within_plane(q, half, state, products, edge, x_ahead, x_behind)
        before = only_behind([below_ref[which][f, 0] for f in span], 3)
        after = only_ahead([above_ref[f, which, 0] for f in span], 3)
        out = [advanced(start_ref[f, which, 0], q[f], sums[f] + before[f] + after[f]) for f in span]
        return state_of(out)[1]

    def fill(ref, which):
        ref[pl.ds(0, older * rows), :] = older_ref[:, which].astype(jnp.float32).reshape(older * rows, lanes)
        ref[pl.ds(older * rows, rows), :] = newest(which)

    def product(parts):
        matrix = jnp.concatenate(parts, axis=1)
        return lax.dot_general(
            matrix, matrix, (((1,), (1,)), ((), ())), preferred_element_type=jnp.float32
        )

    last = parts_of(odd_ref)
    fill(even_ref, 0)
    total_ref[...] += product(last + parts_of(even_ref))
    fill(odd_ref, 1)

    @pl.when(step == pl.num_programs(0) - 1)
    def _():
        total = total_ref[...] + product(parts_of(odd_ref))
        half = snaps // 2
        first, final = total[:half, :half], total[half:, half:]
        r, c = iota((half, half), 0), iota((half, half), 1)
        folded_ref[:half] = jnp.where(r <= c, first, final)
        folded_ref[half : 2 * half] = total[:half, half:]
        diagonal = jnp.sum(jnp.where(r == c, final, 0.0), axis=0, keepdims=True)
        folded_ref[2 * half :] = jnp.broadcast_to(diagonal, (folded_ref.shape[0] - 2 * half, half))
        size = mine_ref.shape[0]
        side = lax.rem(lax.axis_index(axis), 2)
        mine_ref[...] = folded_ref[pl.ds(pl.multiple_of(side * size, 8), size), :]
        sent_ref[...] = folded_ref[pl.ds(pl.multiple_of((1 - side) * size, 8), size), :]


def gram(history, now, start, left, right, xlo, xhi, axis):
    older, samples, rows, lanes = history.shape
    fields, planes = now.shape[:2]
    snaps = older + 1
    half = snaps // 2
    pair = 2
    size = half + 8
    samples_of = (fields, pair, ZSUB, rows, lanes)
    grouped = (fields, samples, ZSUB, rows, lanes)

    def below(which):
        return pl.BlockSpec(
            (fields, 1, rows, lanes),
            lambda p: (0, jnp.maximum(ZSUB * (pair * p + which) - 1, 0), 0, 0),
        )

    def plane(offset):
        return pl.BlockSpec((fields, pair, 1, rows, lanes), lambda p: (0, p, offset, 0, 0))

    whole = pl.BlockSpec((fields, rows, lanes), lambda p: (0, 0, 0))
    line = pl.BlockSpec((fields, planes, lanes), lambda p: (0, 0, 0))
    result = pl.BlockSpec((size, half), lambda p: (0, 0))

    def body(older_ref, below_0, below_1, *refs):
        gram_body(older_ref, (below_0, below_1), *refs, axis=axis)

    return pl.pallas_call(
        body,
        out_shape=(jax.ShapeDtypeStruct((size, half), jnp.float32),) * 2,
        grid=(samples // pair,),
        in_specs=[
            pl.BlockSpec((older, pair, rows, lanes), lambda p: (0, p, 0, 0)),
            below(0), below(1), plane(0), plane(1), plane(0), whole, whole, line, line,
        ],
        out_specs=(result, result),
        scratch_shapes=[
            pltpu.VMEM((snaps * rows, lanes), jnp.float32),
            pltpu.VMEM((snaps * rows, lanes), jnp.float32),
            pltpu.VMEM((snaps, snaps), jnp.float32),
            pltpu.VMEM((fields, rows, lanes), jnp.float32),
            pltpu.VMEM((2 * size, half), jnp.float32),
        ],
        name="gram",
    )(
        history, now, now, now.reshape(grouped), now.reshape(grouped), start.reshape(grouped),
        left, right, xlo, xhi,
    )


def factor_body(scale, axis, mine_ref, other_ref, out_ref, gram_ref, folded_ref):
    size, half = mine_ref.shape
    side = lax.rem(lax.axis_index(axis), 2)
    folded_ref[pl.ds(pl.multiple_of(side * size, 8), size), :] = mine_ref[...]
    folded_ref[pl.ds(pl.multiple_of((1 - side) * size, 8), size), :] = other_ref[...]
    group = 8
    r, c = iota((half, half), 0), iota((half, half), 1)
    mixed = folded_ref[:half] * scale
    turned = mixed.T
    gram_ref[:half, :half] = jnp.where(r <= c, mixed, turned)
    gram_ref[:half, half:] = folded_ref[half : 2 * half] * scale
    diagonal = jnp.broadcast_to(folded_ref[2 * half : 2 * half + 1] * scale, (half, half))
    gram_ref[half:, half:] = jnp.where(r == c, diagonal, jnp.where(r > c, mixed, turned))
    out_ref[half:, :half] = jnp.zeros((half, half), jnp.float32)
    sub, lane = iota((group, half), 0), iota((group, half), 1)
    span = range(group)

    def column(x, index):
        return jnp.broadcast_to(x[:, index : index + 1], (group, half))

    def line(x, index):
        return jnp.broadcast_to(x[index : index + 1, :], (group, half))

    per = half // group
    for panel in range(2):
        width = 2 - panel
        tiles = [
            [
                gram_ref[pl.ds(panel * half + group * t, group), pl.ds((panel + v) * half, half)]
                for v in range(width)
            ]
            for t in range(per)
        ]
        for t in range(per):
            first = group * t
            own = [column(tiles[t][0], first + j) for j in span]
            pivot = {(i, j): line(own[j], i) for j in span for i in range(j + 1)}
            rows = [[line(x, i) for x in tiles[t]] for i in span]
            later = range(t + 1, per)
            lower = {m: [column(tiles[m][0], first + j) for j in span] for m in later}
            for i in span:
                inverse = lax.rsqrt(pivot[i, i])
                for j in range(i + 1, group):
                    pivot[i, j] = pivot[i, j] * inverse
                for j in range(i + 1, group):
                    for k in range(j, group):
                        pivot[j, k] = pivot[j, k] - pivot[i, j] * pivot[i, k]
                rows[i] = [x * inverse for x in rows[i]]
                for j in range(i + 1, group):
                    rows[j] = [a - pivot[i, j] * b for a, b in zip(rows[j], rows[i])]
                for m in later:
                    entry = lower[m][i] * inverse
                    for j in range(i + 1, group):
                        lower[m][j] = lower[m][j] - entry * pivot[i, j]
                    tiles[m] = [a - entry * b for a, b in zip(tiles[m], rows[i])]
            for v in range(width):
                merged = rows[0][v]
                for i in range(1, group):
                    merged = jnp.where(sub == i, rows[i][v], merged)
                if v == 0:
                    merged = jnp.where(lane >= first + sub, merged, 0.0)
                out_ref[pl.ds(panel * half + first, group), pl.ds((panel + v) * half, half)] = merged
        if panel == 0:
            across = out_ref[:half, half:]
            gram_ref[half:, half:] = gram_ref[half:, half:] - lax.dot_general(
                across,
                across,
                (((0,), (0,)), ((), ())),
                precision=lax.Precision.HIGHEST,
                preferred_element_type=jnp.float32,
            )


def factor(mine, other, rows_total, axis):
    size, half = mine.shape
    in_vmem = pl.BlockSpec(memory_space=pltpu.VMEM)
    return pl.pallas_call(
        functools.partial(factor_body, 1.0 / rows_total, axis),
        out_shape=jax.ShapeDtypeStruct((2 * half, 2 * half), jnp.float32),
        in_specs=[in_vmem, in_vmem],
        out_specs=in_vmem,
        scratch_shapes=[
            pltpu.VMEM((2 * half, 2 * half), jnp.float32),
            pltpu.VMEM((2 * size, half), jnp.float32),
        ],
        name="factor",
    )(mine, other)


def local(section_start, section_now, history):
    axes = ("gx", "gy")
    count = lax.axis_size("gx") * lax.axis_size("gy")
    lo, hi, cols = edges(section_now)

    def shifted(part, axis, by):
        size = lax.axis_size(axis)
        return lax.ppermute(part, axis, [(i, (i + by) % size) for i in range(size)])

    def swap(part, bit):
        return lax.ppermute(part, axes, [(i, i ^ bit) for i in range(count)])

    xlo, xhi = shifted(hi, "gx", 1), shifted(lo, "gx", -1)
    left, right = shifted(cols, "gy", 1), shifted(cols, "gy", -1)
    around = (left, right, xlo, xhi)
    mine, sent = gram(history, section_now, section_start, *around, "gy")
    mine = mine + swap(sent, 1)
    bit = 2
    while bit < count:
        mine = mine + swap(mine, bit)
        bit *= 2
    rows_total = history[0].size * count
    triangle = factor(mine, swap(mine, 1), rows_total, "gy")
    chunks = section_now.shape[1] // CHUNK
    section_next = stencil(section_now, section_start, *around, 0, chunks // 2, None)
    section_next = stencil(section_now, section_start, *around, chunks // 2, chunks - chunks // 2, section_next)
    return (section_next, triangle)


def solution(mesh):
    placed = P(None, None, "gx", "gy")
    return jax.shard_map(
        local,
        mesh=mesh,
        in_specs=(placed, placed, placed),
        out_specs=(placed, P()),
        check_vma=False,
    )
```

```python
import functools

import jax
import jax.numpy as jnp
from jax import lax
from jax.experimental import pallas as pl
from jax.experimental.pallas import tpu as pltpu
from jax.sharding import PartitionSpec as P


ZSUB = 4
GAMMA_LESS = 0.4
TIME_STEP = 0.2
VISCOUS = 0.25
CHUNK = 8
PIECES = 4


def iota(shape, dim):
    return lax.broadcasted_iota(jnp.int32, shape, dim)


def is_even(axis):
    return lax.rem(lax.axis_index(axis), 2) == 0


def edges_body(now_ref, first_ref, second_ref, cols_ref):
    fields, planes, rows, lanes = now_ref.shape
    even = is_even("gx")
    lo, hi = now_ref[:, :, 0, :], now_ref[:, :, rows - 1, :]
    first_ref[...] = jnp.where(even, hi, lo)
    second_ref[...] = jnp.where(even, lo, hi)
    key = lax.rem((iota((rows, lanes), 1) + 1) // 2, planes)
    masks = 8
    for f in range(fields):
        parts = [jnp.zeros((rows, lanes), jnp.float32)] * masks
        for z in range(planes):
            cells = now_ref[f, z]
            rolled = pltpu.roll(cells, 2 * z, 1) if z else cells
            parts[z % masks] = jnp.where(key == z, rolled, parts[z % masks])
        while len(parts) > 1:
            parts = [x + y for x, y in zip(parts[::2], parts[1::2])]
        cols_ref[f] = parts[0]


def edges(now):
    fields, planes, rows, lanes = now.shape
    assert 2 * planes == lanes
    line = jax.ShapeDtypeStruct((fields, planes, lanes), now.dtype)
    in_vmem = pl.BlockSpec(memory_space=pltpu.VMEM)
    return pl.pallas_call(
        edges_body,
        out_shape=(line, line, jax.ShapeDtypeStruct((fields, rows, lanes), now.dtype)),
        in_specs=[in_vmem],
        out_specs=(in_vmem, in_vmem, in_vmem),
        name="edges",
    )(now)


def state_of(q):
    inverse = 1.0 / q[0]
    speed = [q[k] * inverse for k in (1, 2, 3)]
    twice = q[1] * speed[0] + q[2] * speed[1] + q[3] * speed[2]
    return speed, GAMMA_LESS * (q[4] - 0.5 * twice)


def products_of(q, state):
    speed, pressure = state
    total = q[4] + pressure
    shared = {}
    for i in range(3):
        for j in range(i, 3):
            shared[i, j] = q[1 + i] * speed[j]
    return shared, total


def flux_of(q, state, direction, products=None):
    speed, pressure = state
    shared, total = products or products_of(q, state)
    d = direction - 1
    columns = [q[direction]] + [shared[min(i, d), max(i, d)] for i in range(3)] + [total * speed[d]]
    columns[direction] = columns[direction] + pressure
    return columns


def scaled(q):
    return [2.0 * VISCOUS * x for x in q]


def ahead_of(base, flux):
    return [a - b for a, b in zip(base, flux)]


def behind_of(base, flux):
    return [a + b for a, b in zip(base, flux)]


def only_ahead(q, direction):
    return ahead_of(scaled(q), flux_of(q, state_of(q), direction))


def only_behind(q, direction):
    return behind_of(scaled(q), flux_of(q, state_of(q), direction))


def sides(axis, first, second):
    even = is_even(axis)
    below = [jnp.where(even, b, a) for a, b in zip(first, second)]
    above = [jnp.where(even, a, b) for a, b in zip(first, second)]
    return below, above


def y_halo(first, second):
    left, right = sides("gy", first, second)
    ahead, behind = only_ahead(right, 2), only_behind(left, 2)
    even = iota(ahead[0].shape, 1) % 2 == 0
    return [jnp.where(even, a, pltpu.roll(b, 2, 1)) for a, b in zip(ahead, behind)]


def within_plane(q, base, state, products, edge, x_ahead, x_behind):
    rows, lanes = q[0].shape
    row, lane = iota((rows, lanes), 0), iota((rows, lanes), 1)
    y = flux_of(q, state, 2, products)
    x = flux_of(q, state, 1, products)
    y_a, y_b, x_a, x_b = ahead_of(base, y), behind_of(base, y), ahead_of(base, x), behind_of(base, x)
    sums = []
    for f in range(len(q)):
        part = jnp.where(lane == lanes - 1, edge[f], pltpu.roll(y_a[f], lanes - 1, 1))
        part = part + jnp.where(lane == 0, edge[f], pltpu.roll(y_b[f], 1, 1))
        other = jnp.where(row == rows - 1, x_ahead[f], pltpu.roll(x_a[f], rows - 1, 0))
        other = other + jnp.where(row == 0, x_behind[f], pltpu.roll(x_b[f], 1, 0))
        sums.append(part + other)
    return sums


def advanced(start, now, total):
    return 0.75 * start + (0.25 * (1.0 - 6.0 * VISCOUS * TIME_STEP)) * now + (0.125 * TIME_STEP) * total


def stencil_body(first, *refs):
    now_ref, below_ref, above_ref, start_ref, y_a_ref, y_b_ref, x_a_ref, x_b_ref = refs[:8]
    next_ref, halo_ref = refs[-2:]
    fields, chunk, _, lanes = now_ref.shape
    step = pl.program_id(0)
    base = (first + step) * chunk
    span = range(fields)

    @pl.when(step == 0)
    def _():
        packed = y_halo([y_a_ref[f] for f in span], [y_b_ref[f] for f in span])
        for f in span:
            halo_ref[f] = packed[f]

    x_lo, x_hi = sides("gx", [x_a_ref[f] for f in span], [x_b_ref[f] for f in span])
    x_behind = only_behind(x_lo, 1)
    x_ahead = only_ahead(x_hi, 1)
    turn = lax.rem(lanes - 2 * base, lanes)
    halo = [pltpu.roll(halo_ref[f], turn, 1) for f in span]
    before = only_behind([below_ref[f, 0] for f in span], 3)
    pending = None

    def finish(j, ahead):
        for f in span:
            next_ref[f, j] = advanced(start_ref[f, j], now_ref[f, j], pending[f] + ahead[f])

    for j in range(chunk):
        q = [now_ref[f, j] for f in span]
        state = state_of(q)
        products = products_of(q, state)
        half = scaled(q)
        flux = flux_of(q, state, 3, products)
        if pending is not None:
            finish(j - 1, ahead_of(half, flux))
        edge = [pltpu.roll(halo[f], lanes - 1 - 2 * j, 1) for f in span]
        sums = within_plane(
            q, half, state, products, edge,
            [x_ahead[f][j : j + 1] for f in span], [x_behind[f][j : j + 1] for f in span],
        )
        pending = [sums[f] + before[f] for f in span]
        before = behind_of(half, flux)
    finish(chunk - 1, only_ahead([above_ref[f, 0] for f in span], 3))


def stencil(now, start, around, first, count, into):
    fields, planes, rows, lanes = now.shape
    chunk = CHUNK
    whole = pl.BlockSpec((fields, rows, lanes), lambda c: (0, 0, 0))
    part = pl.BlockSpec((fields, chunk, rows, lanes), lambda c: (0, first + c, 0, 0))
    line = pl.BlockSpec((fields, chunk, lanes), lambda c: (0, first + c, 0))
    below = pl.BlockSpec(
        (fields, 1, rows, lanes), lambda c: (0, jnp.maximum((first + c) * chunk - 1, 0), 0, 0)
    )
    above = pl.BlockSpec(
        (fields, 1, rows, lanes), lambda c: (0, jnp.minimum((first + c + 1) * chunk, planes - 1), 0, 0)
    )
    specs = [part, below, above, part, whole, whole, line, line]
    operands = [now, now, now, start, *around]
    if into is not None:
        specs.append(pl.BlockSpec(memory_space=pl.ANY))
        operands.append(into)
    return pl.pallas_call(
        functools.partial(stencil_body, first),
        out_shape=jax.ShapeDtypeStruct(now.shape, now.dtype),
        grid=(count,),
        in_specs=specs,
        out_specs=part,
        scratch_shapes=[pltpu.VMEM((fields, rows, lanes), jnp.float32)],
        input_output_aliases={} if into is None else {len(operands) - 1: 0},
    )(*operands)


def gram_body(
    older_ref, below_ref, now_ref, above_ref, start_ref, y_a_ref, y_b_ref, x_a_ref, x_b_ref,
    mine_ref, sent_ref, even_ref, odd_ref, total_ref, halo_ref, folded_ref, *, axis,
):
    older, pair, rows, lanes = older_ref.shape
    fields = halo_ref.shape[0]
    snaps = total_ref.shape[0]
    step = pl.program_id(0)
    span = range(fields)

    @pl.when(step == 0)
    def _():
        total_ref[...] = jnp.zeros_like(total_ref)
        odd_ref[...] = jnp.zeros_like(odd_ref)
        packed = y_halo([y_a_ref[f] for f in span], [y_b_ref[f] for f in span])
        for f in span:
            halo_ref[f] = packed[f]

    def parts_of(ref):
        return [ref[pl.ds(r, snaps, stride=rows), :].astype(jnp.bfloat16) for r in range(rows)]

    def newest(which):
        z = ZSUB * (pair * step + which)
        q = [now_ref[f, which, 0] for f in span]
        state = state_of(q)
        products = products_of(q, state)
        half = scaled(q)
        turn = lax.rem(2 * lanes - 1 - 2 * z, lanes)
        edge = [pltpu.roll(halo_ref[f], turn, 1) for f in span]
        x_lo, x_hi = sides(
            "gx", [x_a_ref[f, pl.ds(z, 1), :] for f in span], [x_b_ref[f, pl.ds(z, 1), :] for f in span]
        )
        x_behind, x_ahead = only_behind(x_lo, 1), only_ahead(x_hi, 1)
        sums = within_plane(q, half, state, products, edge, x_ahead, x_behind)
        before = only_behind([below_ref[which][f, 0] for f in span], 3)
        after = only_ahead([above_ref[f, which, 0] for f in span], 3)
        out = [advanced(start_ref[f, which, 0], q[f], sums[f] + before[f] + after[f]) for f in span]
        return state_of(out)[1]

    def fill(ref, which):
        ref[pl.ds(0, older * rows), :] = older_ref[:, which].astype(jnp.float32).reshape(older * rows, lanes)
        ref[pl.ds(older * rows, rows), :] = newest(which)

    def product(parts):
        matrix = jnp.concatenate(parts, axis=1)
        return lax.dot_general(
            matrix, matrix, (((1,), (1,)), ((), ())), preferred_element_type=jnp.float32
        )

    last = parts_of(odd_ref)
    fill(even_ref, 0)
    total_ref[...] += product(last + parts_of(even_ref))
    fill(odd_ref, 1)

    @pl.when(step == pl.num_programs(0) - 1)
    def _():
        total = total_ref[...] + product(parts_of(odd_ref))
        half = snaps // 2
        first, final = total[:half, :half], total[half:, half:]
        r, c = iota((half, half), 0), iota((half, half), 1)
        folded_ref[:half] = jnp.where(r <= c, first, final)
        folded_ref[half : 2 * half] = total[:half, half:]
        diagonal = jnp.sum(jnp.where(r == c, final, 0.0), axis=0, keepdims=True)
        folded_ref[2 * half :] = jnp.broadcast_to(diagonal, (folded_ref.shape[0] - 2 * half, half))
        size = mine_ref.shape[0]
        side = lax.rem(lax.axis_index(axis), 2)
        mine_ref[...] = folded_ref[pl.ds(pl.multiple_of(side * size, 8), size), :]
        sent_ref[...] = folded_ref[pl.ds(pl.multiple_of((1 - side) * size, 8), size), :]


def gram(history, now, start, around, axis):
    older, samples, rows, lanes = history.shape
    fields, planes = now.shape[:2]
    snaps = older + 1
    half = snaps // 2
    pair = 2
    size = half + 8
    grouped = (fields, samples, ZSUB, rows, lanes)

    def below(which):
        return pl.BlockSpec(
            (fields, 1, rows, lanes),
            lambda p: (0, jnp.maximum(ZSUB * (pair * p + which) - 1, 0), 0, 0),
        )

    def plane(offset):
        return pl.BlockSpec((fields, pair, 1, rows, lanes), lambda p: (0, p, offset, 0, 0))

    whole = pl.BlockSpec((fields, rows, lanes), lambda p: (0, 0, 0))
    line = pl.BlockSpec((fields, planes, lanes), lambda p: (0, 0, 0))
    result = pl.BlockSpec((size, half), lambda p: (0, 0))

    def body(older_ref, below_0, below_1, *refs):
        gram_body(older_ref, (below_0, below_1), *refs, axis=axis)

    return pl.pallas_call(
        body,
        out_shape=(jax.ShapeDtypeStruct((size, half), jnp.float32),) * 2,
        grid=(samples // pair,),
        in_specs=[
            pl.BlockSpec((older, pair, rows, lanes), lambda p: (0, p, 0, 0)),
            below(0), below(1), plane(0), plane(1), plane(0), whole, whole, line, line,
        ],
        out_specs=(result, result),
        scratch_shapes=[
            pltpu.VMEM((snaps * rows, lanes), jnp.float32),
            pltpu.VMEM((snaps * rows, lanes), jnp.float32),
            pltpu.VMEM((snaps, snaps), jnp.float32),
            pltpu.VMEM((fields, rows, lanes), jnp.float32),
            pltpu.VMEM((2 * size, half), jnp.float32),
        ],
        name="gram",
    )(
        history, now, now, now.reshape(grouped), now.reshape(grouped), start.reshape(grouped), *around
    )


def factor_body(scale, axis, mine_ref, other_ref, out_ref, gram_ref, folded_ref):
    size, half = mine_ref.shape
    side = lax.rem(lax.axis_index(axis), 2)
    folded_ref[pl.ds(pl.multiple_of(side * size, 8), size), :] = mine_ref[...]
    folded_ref[pl.ds(pl.multiple_of((1 - side) * size, 8), size), :] = other_ref[...]
    group = 8
    r, c = iota((half, half), 0), iota((half, half), 1)
    mixed = folded_ref[:half] * scale
    turned = mixed.T
    gram_ref[:half, :half] = jnp.where(r <= c, mixed, turned)
    gram_ref[:half, half:] = folded_ref[half : 2 * half] * scale
    diagonal = jnp.broadcast_to(folded_ref[2 * half : 2 * half + 1] * scale, (half, half))
    gram_ref[half:, half:] = jnp.where(r == c, diagonal, jnp.where(r > c, mixed, turned))
    out_ref[half:, :half] = jnp.zeros((half, half), jnp.float32)
    sub, lane = iota((group, half), 0), iota((group, half), 1)
    span = range(group)

    def column(x, index):
        return jnp.broadcast_to(x[:, index : index + 1], (group, half))

    def line(x, index):
        return jnp.broadcast_to(x[index : index + 1, :], (group, half))

    per = half // group
    for panel in range(2):
        width = 2 - panel
        tiles = [
            [
                gram_ref[pl.ds(panel * half + group * t, group), pl.ds((panel + v) * half, half)]
                for v in range(width)
            ]
            for t in range(per)
        ]
        for t in range(per):
            first = group * t
            own = [column(tiles[t][0], first + j) for j in span]
            pivot = {(i, j): line(own[j], i) for j in span for i in range(j + 1)}
            rows = [[line(x, i) for x in tiles[t]] for i in span]
            later = range(t + 1, per)
            lower = {m: [column(tiles[m][0], first + j) for j in span] for m in later}
            for i in span:
                inverse = lax.rsqrt(pivot[i, i])
                for j in range(i + 1, group):
                    pivot[i, j] = pivot[i, j] * inverse
                for j in range(i + 1, group):
                    for k in range(j, group):
                        pivot[j, k] = pivot[j, k] - pivot[i, j] * pivot[i, k]
                rows[i] = [x * inverse for x in rows[i]]
                for j in range(i + 1, group):
                    rows[j] = [a - pivot[i, j] * b for a, b in zip(rows[j], rows[i])]
                for m in later:
                    entry = lower[m][i] * inverse
                    for j in range(i + 1, group):
                        lower[m][j] = lower[m][j] - entry * pivot[i, j]
                    tiles[m] = [a - entry * b for a, b in zip(tiles[m], rows[i])]
            for v in range(width):
                merged = rows[0][v]
                for i in range(1, group):
                    merged = jnp.where(sub == i, rows[i][v], merged)
                if v == 0:
                    merged = jnp.where(lane >= first + sub, merged, 0.0)
                out_ref[pl.ds(panel * half + first, group), pl.ds((panel + v) * half, half)] = merged
        if panel == 0:
            across = out_ref[:half, half:]
            gram_ref[half:, half:] = gram_ref[half:, half:] - lax.dot_general(
                across,
                across,
                (((0,), (0,)), ((), ())),
                precision=lax.Precision.HIGHEST,
                preferred_element_type=jnp.float32,
            )


def factor(mine, other, rows_total, axis):
    size, half = mine.shape
    in_vmem = pl.BlockSpec(memory_space=pltpu.VMEM)
    return pl.pallas_call(
        functools.partial(factor_body, 1.0 / rows_total, axis),
        out_shape=jax.ShapeDtypeStruct((2 * half, 2 * half), jnp.float32),
        in_specs=[in_vmem, in_vmem],
        out_specs=in_vmem,
        scratch_shapes=[
            pltpu.VMEM((2 * half, 2 * half), jnp.float32),
            pltpu.VMEM((2 * size, half), jnp.float32),
        ],
        name="factor",
    )(mine, other)


def local(section_start, section_now, history):
    axes = ("gx", "gy")
    count = lax.axis_size("gx") * lax.axis_size("gy")
    first, second, cols = edges(section_now)

    def neighbours(part, axis, by):
        size = lax.axis_size(axis)
        assert size % 2 == 0
        return lax.ppermute(part, axis, [(i, (i + by * (-1) ** i) % size) for i in range(size)])

    def swap(part, bit):
        return lax.ppermute(part, axes, [(i, i ^ bit) for i in range(count)])

    x_a, x_b = neighbours(first, "gx", 1), neighbours(second, "gx", -1)
    y_a, y_b = neighbours(cols, "gy", 1), neighbours(cols, "gy", -1)
    around = (y_a, y_b, x_a, x_b)
    mine, sent = gram(history, section_now, section_start, around, "gy")
    mine = mine + swap(sent, 1)
    bit = 2
    while bit < count:
        mine = mine + swap(mine, bit)
        bit *= 2
    rows_total = history[0].size * count
    triangle = factor(mine, swap(mine, 1), rows_total, "gy")
    chunks = section_now.shape[1] // CHUNK
    section_next = None
    for piece in range(PIECES):
        low, high = piece * chunks // PIECES, (piece + 1) * chunks // PIECES
        section_next = stencil(section_now, section_start, around, low, high - low, section_next)
    return (section_next, triangle)


def solution(mesh):
    placed = P(None, None, "gx", "gy")
    return jax.shard_map(
        local,
        mesh=mesh,
        in_specs=(placed, placed, placed),
        out_specs=(placed, P()),
        check_vma=False,
    )
```

```python
import functools

import jax
import jax.numpy as jnp
from jax import lax
from jax.experimental import pallas as pl
from jax.experimental.pallas import tpu as pltpu
from jax.sharding import PartitionSpec as P


ZSUB = 4
GAMMA_LESS = 0.4
TIME_STEP = 0.2
VISCOUS = 0.25
CHUNK = 8
PIECES = 4


def iota(shape, dim):
    return lax.broadcasted_iota(jnp.int32, shape, dim)


def is_even(axis):
    return lax.rem(lax.axis_index(axis), 2) == 0


def edges_body(now_ref, first_ref, second_ref, cols_ref):
    fields, planes, rows, lanes = now_ref.shape
    even = is_even("gx")
    lo, hi = now_ref[:, :, 0, :], now_ref[:, :, rows - 1, :]
    first_ref[...] = jnp.where(even, hi, lo)
    second_ref[...] = jnp.where(even, lo, hi)
    key = lax.rem((iota((rows, lanes), 1) + 1) // 2, planes)
    masks = 8
    for f in range(fields):
        parts = [jnp.zeros((rows, lanes), jnp.float32)] * masks
        for z in range(planes):
            cells = now_ref[f, z]
            rolled = pltpu.roll(cells, 2 * z, 1) if z else cells
            parts[z % masks] = jnp.where(key == z, rolled, parts[z % masks])
        while len(parts) > 1:
            parts = [x + y for x, y in zip(parts[::2], parts[1::2])]
        cols_ref[f] = parts[0]


def edges(now):
    fields, planes, rows, lanes = now.shape
    assert 2 * planes == lanes
    line = jax.ShapeDtypeStruct((fields, planes, lanes), now.dtype)
    in_vmem = pl.BlockSpec(memory_space=pltpu.VMEM)
    return pl.pallas_call(
        edges_body,
        out_shape=(line, line, jax.ShapeDtypeStruct((fields, rows, lanes), now.dtype)),
        in_specs=[in_vmem],
        out_specs=(in_vmem, in_vmem, in_vmem),
        name="edges",
    )(now)


def state_of(q):
    inverse = 1.0 / q[0]
    speed = [q[k] * inverse for k in (1, 2, 3)]
    twice = q[1] * speed[0] + q[2] * speed[1] + q[3] * speed[2]
    return speed, GAMMA_LESS * (q[4] - 0.5 * twice)


def products_of(q, state):
    speed, pressure = state
    total = q[4] + pressure
    shared = {}
    for i in range(3):
        for j in range(i, 3):
            shared[i, j] = q[1 + i] * speed[j]
    return shared, total


def flux_of(q, state, direction, products=None):
    speed, pressure = state
    shared, total = products or products_of(q, state)
    d = direction - 1
    columns = [q[direction]] + [shared[min(i, d), max(i, d)] for i in range(3)] + [total * speed[d]]
    columns[direction] = columns[direction] + pressure
    return columns


def scaled(q):
    return [2.0 * VISCOUS * x for x in q]


def ahead_of(base, flux):
    return [a - b for a, b in zip(base, flux)]


def behind_of(base, flux):
    return [a + b for a, b in zip(base, flux)]


def only_ahead(q, direction):
    return ahead_of(scaled(q), flux_of(q, state_of(q), direction))


def only_behind(q, direction):
    return behind_of(scaled(q), flux_of(q, state_of(q), direction))


def sides(axis, first, second):
    even = is_even(axis)
    below = [jnp.where(even, b, a) for a, b in zip(first, second)]
    above = [jnp.where(even, a, b) for a, b in zip(first, second)]
    return below, above


def y_halo(first, second):
    left, right = sides("gy", first, second)
    ahead, behind = only_ahead(right, 2), only_behind(left, 2)
    even = iota(ahead[0].shape, 1) % 2 == 0
    return [jnp.where(even, a, pltpu.roll(b, 2, 1)) for a, b in zip(ahead, behind)]


def within_plane(q, base, state, products, edge, x_ahead, x_behind):
    rows, lanes = q[0].shape
    row, lane = iota((rows, lanes), 0), iota((rows, lanes), 1)
    y = flux_of(q, state, 2, products)
    x = flux_of(q, state, 1, products)
    y_a, y_b, x_a, x_b = ahead_of(base, y), behind_of(base, y), ahead_of(base, x), behind_of(base, x)
    sums = []
    for f in range(len(q)):
        part = jnp.where(lane == lanes - 1, edge[f], pltpu.roll(y_a[f], lanes - 1, 1))
        part = part + jnp.where(lane == 0, edge[f], pltpu.roll(y_b[f], 1, 1))
        other = jnp.where(row == rows - 1, x_ahead[f], pltpu.roll(x_a[f], rows - 1, 0))
        other = other + jnp.where(row == 0, x_behind[f], pltpu.roll(x_b[f], 1, 0))
        sums.append(part + other)
    return sums


def advanced(start, now, total):
    return 0.75 * start + (0.25 * (1.0 - 6.0 * VISCOUS * TIME_STEP)) * now + (0.125 * TIME_STEP) * total


def stencil_body(first, *refs):
    now_ref, below_ref, above_ref, start_ref, y_a_ref, y_b_ref, x_a_ref, x_b_ref = refs[:8]
    next_ref, halo_ref = refs[-2:]
    fields, chunk, _, lanes = now_ref.shape
    step = pl.program_id(0)
    base = (first + step) * chunk
    span = range(fields)

    @pl.when(step == 0)
    def _():
        packed = y_halo([y_a_ref[f] for f in span], [y_b_ref[f] for f in span])
        for f in span:
            halo_ref[f] = packed[f]

    x_lo, x_hi = sides("gx", [x_a_ref[f] for f in span], [x_b_ref[f] for f in span])
    x_behind = only_behind(x_lo, 1)
    x_ahead = only_ahead(x_hi, 1)
    turn = lax.rem(lanes - 2 * base, lanes)
    halo = [pltpu.roll(halo_ref[f], turn, 1) for f in span]
    before = only_behind([below_ref[f, 0] for f in span], 3)
    pending = None

    def finish(j, ahead):
        for f in span:
            next_ref[f, j] = advanced(start_ref[f, j], now_ref[f, j], pending[f] + ahead[f])

    for j in range(chunk):
        q = [now_ref[f, j] for f in span]
        state = state_of(q)
        products = products_of(q, state)
        half = scaled(q)
        flux = flux_of(q, state, 3, products)
        if pending is not None:
            finish(j - 1, ahead_of(half, flux))
        edge = [pltpu.roll(halo[f], lanes - 1 - 2 * j, 1) for f in span]
        sums = within_plane(
            q, half, state, products, edge,
            [x_ahead[f][j : j + 1] for f in span], [x_behind[f][j : j + 1] for f in span],
        )
        pending = [sums[f] + before[f] for f in span]
        before = behind_of(half, flux)
    finish(chunk - 1, only_ahead([above_ref[f, 0] for f in span], 3))


def stencil(now, start, around, first, count, into):
    fields, planes, rows, lanes = now.shape
    chunk = CHUNK
    whole = pl.BlockSpec((fields, rows, lanes), lambda c: (0, 0, 0))
    part = pl.BlockSpec((fields, chunk, rows, lanes), lambda c: (0, first + c, 0, 0))
    line = pl.BlockSpec((fields, chunk, lanes), lambda c: (0, first + c, 0))
    below = pl.BlockSpec(
        (fields, 1, rows, lanes), lambda c: (0, jnp.maximum((first + c) * chunk - 1, 0), 0, 0)
    )
    above = pl.BlockSpec(
        (fields, 1, rows, lanes), lambda c: (0, jnp.minimum((first + c + 1) * chunk, planes - 1), 0, 0)
    )
    specs = [part, below, above, part, whole, whole, line, line]
    operands = [now, now, now, start, *around]
    if into is not None:
        specs.append(pl.BlockSpec(memory_space=pl.ANY))
        operands.append(into)
    return pl.pallas_call(
        functools.partial(stencil_body, first),
        out_shape=jax.ShapeDtypeStruct(now.shape, now.dtype),
        grid=(count,),
        in_specs=specs,
        out_specs=part,
        scratch_shapes=[pltpu.VMEM((fields, rows, lanes), jnp.float32)],
        input_output_aliases={} if into is None else {len(operands) - 1: 0},
    )(*operands)


def relayout_body(older_ref, out_ref, *cells_refs):
    older, _, rows, lanes = older_ref.shape
    snaps = out_ref.shape[1]

    @pl.when(pl.program_id(0) == 0)
    def _():
        for ref in cells_refs:
            ref[pl.ds(older * rows, (snaps - older) * rows), :] = jnp.zeros(
                ((snaps - older) * rows, lanes), jnp.float32
            )

    for which, ref in enumerate(cells_refs):
        ref[pl.ds(0, older * rows), :] = older_ref[:, which].astype(jnp.float32).reshape(older * rows, lanes)
    for which, ref in enumerate(cells_refs):
        for r in range(rows):
            part = ref[pl.ds(r, snaps, stride=rows), :]
            out_ref[which, :, r * lanes : (r + 1) * lanes] = part.astype(out_ref.dtype)


def relayout(history):
    older, samples, rows, lanes = history.shape
    snaps = older + 1
    pair = 2
    return pl.pallas_call(
        relayout_body,
        out_shape=jax.ShapeDtypeStruct((samples, snaps, rows * lanes), history.dtype),
        grid=(samples // pair,),
        in_specs=[pl.BlockSpec((older, pair, rows, lanes), lambda p: (0, p, 0, 0))],
        out_specs=pl.BlockSpec((pair, snaps, rows * lanes), lambda p: (p, 0, 0)),
        scratch_shapes=[pltpu.VMEM((snaps * rows, lanes), jnp.float32)] * pair,
        name="relayout",
    )(history)


def gram_body(
    cells_ref, below_refs, now_ref, above_ref, start_ref, y_a_ref, y_b_ref, x_a_ref, x_b_ref,
    mine_ref, sent_ref, newest_ref, total_ref, halo_ref, folded_ref, *, axis,
):
    pair, snaps, width = cells_ref.shape
    fields, rows, lanes = halo_ref.shape
    step = pl.program_id(0)
    groups = pl.num_programs(0) - 1
    span = range(fields)
    tile = 16

    @pl.when(step == 0)
    def _():
        newest_ref[...] = jnp.zeros_like(newest_ref)
        packed = y_halo([y_a_ref[f] for f in span], [y_b_ref[f] for f in span])
        for f in span:
            halo_ref[f] = packed[f]

    bottom = iota((tile, width), 0) == tile - 1
    parts = []
    for which in range(pair):
        row = jnp.concatenate([newest_ref[which, r : r + 1, :] for r in range(rows)], axis=1)
        last = cells_ref[which, snaps - tile :, :].astype(jnp.float32)
        last = jnp.where(bottom, row, last).astype(cells_ref.dtype)
        parts.append(jnp.concatenate([cells_ref[which, : snaps - tile, :], last], axis=0))
    matrix = jnp.concatenate(parts, axis=1)
    product = lax.dot_general(
        matrix, matrix, (((1,), (1,)), ((), ())), preferred_element_type=jnp.float32
    )

    def newest(which):
        z = ZSUB * (pair * jnp.minimum(step, groups - 1) + which)
        q = [now_ref[f, which, 0] for f in span]
        state = state_of(q)
        products = products_of(q, state)
        half = scaled(q)
        turn = lax.rem(2 * lanes - 1 - 2 * z, lanes)
        edge = [pltpu.roll(halo_ref[f], turn, 1) for f in span]
        x_lo, x_hi = sides(
            "gx", [x_a_ref[f, pl.ds(z, 1), :] for f in span], [x_b_ref[f, pl.ds(z, 1), :] for f in span]
        )
        x_behind, x_ahead = only_behind(x_lo, 1), only_ahead(x_hi, 1)
        sums = within_plane(q, half, state, products, edge, x_ahead, x_behind)
        before = only_behind([below_refs[which][f, 0] for f in span], 3)
        after = only_ahead([above_ref[f, which, 0] for f in span], 3)
        out = [advanced(start_ref[f, which, 0], q[f], sums[f] + before[f] + after[f]) for f in span]
        return state_of(out)[1]

    fresh = [newest(which) for which in range(pair)]
    for which in range(pair):
        newest_ref[which] = fresh[which]
    total_ref[...] = jnp.where(step > 1, total_ref[...], 0.0) + product

    @pl.when(step == groups)
    def _():
        half = snaps // 2
        first, final = total_ref[:half, :half], total_ref[half:, half:]
        r, c = iota((half, half), 0), iota((half, half), 1)
        folded_ref[:half] = jnp.where(r <= c, first, final)
        folded_ref[half : 2 * half] = total_ref[:half, half:]
        diagonal = jnp.sum(jnp.where(r == c, final, 0.0), axis=0, keepdims=True)
        folded_ref[2 * half :] = jnp.broadcast_to(diagonal, (folded_ref.shape[0] - 2 * half, half))
        size = mine_ref.shape[0]
        side = lax.rem(lax.axis_index(axis), 2)
        mine_ref[...] = folded_ref[pl.ds(pl.multiple_of(side * size, 8), size), :]
        sent_ref[...] = folded_ref[pl.ds(pl.multiple_of((1 - side) * size, 8), size), :]


def gram(cells, now, start, around, axis):
    samples, snaps, width = cells.shape
    fields, _, rows, lanes = now.shape
    half = snaps // 2
    pair = 2
    groups = samples // pair
    size = half + 8
    grouped = (fields, samples, ZSUB, rows, lanes)

    def here(p):
        return jnp.minimum(p, groups - 1)

    def below(which):
        return pl.BlockSpec(
            (fields, 1, rows, lanes),
            lambda p: (0, jnp.maximum(ZSUB * (pair * here(p) + which) - 1, 0), 0, 0),
        )

    def plane(offset):
        return pl.BlockSpec((fields, pair, 1, rows, lanes), lambda p: (0, here(p), offset, 0, 0))

    in_vmem = pl.BlockSpec(memory_space=pltpu.VMEM)
    result = pl.BlockSpec((size, half), lambda p: (0, 0))

    def body(cells_ref, below_0, below_1, *refs):
        gram_body(cells_ref, (below_0, below_1), *refs, axis=axis)

    return pl.pallas_call(
        body,
        out_shape=(jax.ShapeDtypeStruct((size, half), jnp.float32),) * 2,
        grid=(groups + 1,),
        in_specs=[
            pl.BlockSpec((pair, snaps, width), lambda p: (jnp.maximum(p - 1, 0), 0, 0)),
            below(0), below(1), plane(0), plane(1), plane(0), in_vmem, in_vmem, in_vmem, in_vmem,
        ],
        out_specs=(result, result),
        scratch_shapes=[
            pltpu.VMEM((pair, rows, lanes), jnp.float32),
            pltpu.VMEM((snaps, snaps), jnp.float32),
            pltpu.VMEM((fields, rows, lanes), jnp.float32),
            pltpu.VMEM((2 * size, half), jnp.float32),
        ],
        name="gram",
    )(
        cells, now, now, now.reshape(grouped), now.reshape(grouped), start.reshape(grouped), *around
    )


def factor_body(scale, axis, mine_ref, other_ref, out_ref, gram_ref, folded_ref):
    size, half = mine_ref.shape
    side = lax.rem(lax.axis_index(axis), 2)
    folded_ref[pl.ds(pl.multiple_of(side * size, 8), size), :] = mine_ref[...]
    folded_ref[pl.ds(pl.multiple_of((1 - side) * size, 8), size), :] = other_ref[...]
    group = 8
    r, c = iota((half, half), 0), iota((half, half), 1)
    mixed = folded_ref[:half] * scale
    turned = mixed.T
    gram_ref[:half, :half] = jnp.where(r <= c, mixed, turned)
    gram_ref[:half, half:] = folded_ref[half : 2 * half] * scale
    diagonal = jnp.broadcast_to(folded_ref[2 * half : 2 * half + 1] * scale, (half, half))
    gram_ref[half:, half:] = jnp.where(r == c, diagonal, jnp.where(r > c, mixed, turned))
    out_ref[half:, :half] = jnp.zeros((half, half), jnp.float32)
    sub, lane = iota((group, half), 0), iota((group, half), 1)
    span = range(group)

    def column(x, index):
        return jnp.broadcast_to(x[:, index : index + 1], (group, half))

    def line(x, index):
        return jnp.broadcast_to(x[index : index + 1, :], (group, half))

    per = half // group
    for panel in range(2):
        width = 2 - panel
        tiles = [
            [
                gram_ref[pl.ds(panel * half + group * t, group), pl.ds((panel + v) * half, half)]
                for v in range(width)
            ]
            for t in range(per)
        ]
        for t in range(per):
            first = group * t
            own = [column(tiles[t][0], first + j) for j in span]
            pivot = {(i, j): line(own[j], i) for j in span for i in range(j + 1)}
            rows = [[line(x, i) for x in tiles[t]] for i in span]
            later = range(t + 1, per)
            lower = {m: [column(tiles[m][0], first + j) for j in span] for m in later}
            for i in span:
                inverse = lax.rsqrt(pivot[i, i])
                for j in range(i + 1, group):
                    pivot[i, j] = pivot[i, j] * inverse
                for j in range(i + 1, group):
                    for k in range(j, group):
                        pivot[j, k] = pivot[j, k] - pivot[i, j] * pivot[i, k]
                rows[i] = [x * inverse for x in rows[i]]
                for j in range(i + 1, group):
                    rows[j] = [a - pivot[i, j] * b for a, b in zip(rows[j], rows[i])]
                for m in later:
                    entry = lower[m][i] * inverse
                    for j in range(i + 1, group):
                        lower[m][j] = lower[m][j] - entry * pivot[i, j]
                    tiles[m] = [a - entry * b for a, b in zip(tiles[m], rows[i])]
            for v in range(width):
                merged = rows[0][v]
                for i in range(1, group):
                    merged = jnp.where(sub == i, rows[i][v], merged)
                if v == 0:
                    merged = jnp.where(lane >= first + sub, merged, 0.0)
                out_ref[pl.ds(panel * half + first, group), pl.ds((panel + v) * half, half)] = merged
        if panel == 0:
            across = out_ref[:half, half:]
            gram_ref[half:, half:] = gram_ref[half:, half:] - lax.dot_general(
                across,
                across,
                (((0,), (0,)), ((), ())),
                precision=lax.Precision.HIGHEST,
                preferred_element_type=jnp.float32,
            )


def factor(mine, other, rows_total, axis):
    size, half = mine.shape
    in_vmem = pl.BlockSpec(memory_space=pltpu.VMEM)
    return pl.pallas_call(
        functools.partial(factor_body, 1.0 / rows_total, axis),
        out_shape=jax.ShapeDtypeStruct((2 * half, 2 * half), jnp.float32),
        in_specs=[in_vmem, in_vmem],
        out_specs=in_vmem,
        scratch_shapes=[
            pltpu.VMEM((2 * half, 2 * half), jnp.float32),
            pltpu.VMEM((2 * size, half), jnp.float32),
        ],
        name="factor",
    )(mine, other)


def local(section_start, section_now, history):
    axes = ("gx", "gy")
    count = lax.axis_size("gx") * lax.axis_size("gy")
    first, second, cols = edges(section_now)

    def neighbours(part, axis, by):
        size = lax.axis_size(axis)
        assert size % 2 == 0
        return lax.ppermute(part, axis, [(i, (i + by * (-1) ** i) % size) for i in range(size)])

    def swap(part, bit):
        return lax.ppermute(part, axes, [(i, i ^ bit) for i in range(count)])

    x_a, x_b = neighbours(first, "gx", 1), neighbours(second, "gx", -1)
    y_a, y_b = neighbours(cols, "gy", 1), neighbours(cols, "gy", -1)
    around = (y_a, y_b, x_a, x_b)
    cells = relayout(history)
    mine, sent = gram(cells, section_now, section_start, around, "gy")
    mine = mine + swap(sent, 1)
    bit = 2
    while bit < count:
        mine = mine + swap(mine, bit)
        bit *= 2
    rows_total = history[0].size * count
    triangle = factor(mine, swap(mine, 1), rows_total, "gy")
    chunks = section_now.shape[1] // CHUNK
    section_next = None
    for piece in range(PIECES):
        low, high = piece * chunks // PIECES, (piece + 1) * chunks // PIECES
        section_next = stencil(section_now, section_start, around, low, high - low, section_next)
    return (section_next, triangle)


def solution(mesh):
    placed = P(None, None, "gx", "gy")
    return jax.shard_map(
        local,
        mesh=mesh,
        in_specs=(placed, placed, placed),
        out_specs=(placed, P()),
        check_vma=False,
    )
```

```python
import functools

import jax
import jax.numpy as jnp
from jax import lax
from jax.experimental import pallas as pl
from jax.experimental.pallas import tpu as pltpu
from jax.sharding import PartitionSpec as P


ZSUB = 4
GAMMA_LESS = 0.4
TIME_STEP = 0.2
VISCOUS = 0.25
CHUNK = 8
PIECES = 4
IN_VMEM = pl.BlockSpec(memory_space=pltpu.VMEM)
ROOM = pltpu.CompilerParams(vmem_limit_bytes=20 * 1024 * 1024)


def iota(shape, dim):
    return lax.broadcasted_iota(jnp.int32, shape, dim)


def is_even(axis):
    return lax.rem(lax.axis_index(axis), 2) == 0


def edges_body(now_ref, first_ref, second_ref, cols_ref):
    fields, planes, rows, lanes = now_ref.shape
    even = is_even("gx")
    lo, hi = now_ref[:, :, 0, :], now_ref[:, :, rows - 1, :]
    first_ref[...] = jnp.where(even, hi, lo)
    second_ref[...] = jnp.where(even, lo, hi)
    key = lax.rem((iota((rows, lanes), 1) + 1) // 2, planes)
    masks = 8
    for f in range(fields):
        parts = [jnp.zeros((rows, lanes), jnp.float32)] * masks
        for z in range(planes):
            cells = now_ref[f, z]
            rolled = pltpu.roll(cells, 2 * z, 1) if z else cells
            parts[z % masks] = jnp.where(key == z, rolled, parts[z % masks])
        while len(parts) > 1:
            parts = [x + y for x, y in zip(parts[::2], parts[1::2])]
        cols_ref[f] = parts[0]


def edges(now):
    fields, planes, rows, lanes = now.shape
    assert 2 * planes == lanes
    line = jax.ShapeDtypeStruct((fields, planes, lanes), now.dtype)
    return pl.pallas_call(
        edges_body,
        out_shape=(line, line, jax.ShapeDtypeStruct((fields, rows, lanes), now.dtype)),
        in_specs=[IN_VMEM],
        out_specs=(IN_VMEM, IN_VMEM, IN_VMEM),
        compiler_params=ROOM,
        name="edges",
    )(now)


def state_of(q):
    inverse = 1.0 / q[0]
    speed = [q[k] * inverse for k in (1, 2, 3)]
    twice = q[1] * speed[0] + q[2] * speed[1] + q[3] * speed[2]
    return speed, GAMMA_LESS * (q[4] - 0.5 * twice)


def products_of(q, state):
    speed, pressure = state
    total = q[4] + pressure
    shared = {}
    for i in range(3):
        for j in range(i, 3):
            shared[i, j] = q[1 + i] * speed[j]
    return shared, total


def flux_of(q, state, direction, products=None):
    speed, pressure = state
    shared, total = products or products_of(q, state)
    d = direction - 1
    columns = [q[direction]] + [shared[min(i, d), max(i, d)] for i in range(3)] + [total * speed[d]]
    columns[direction] = columns[direction] + pressure
    return columns


def scaled(q):
    return [2.0 * VISCOUS * x for x in q]


def ahead_of(base, flux):
    return [a - b for a, b in zip(base, flux)]


def behind_of(base, flux):
    return [a + b for a, b in zip(base, flux)]


def only_ahead(q, direction):
    return ahead_of(scaled(q), flux_of(q, state_of(q), direction))


def only_behind(q, direction):
    return behind_of(scaled(q), flux_of(q, state_of(q), direction))


def sides(axis, first, second):
    even = is_even(axis)
    below = [jnp.where(even, b, a) for a, b in zip(first, second)]
    above = [jnp.where(even, a, b) for a, b in zip(first, second)]
    return below, above


def y_halo(first, second):
    left, right = sides("gy", first, second)
    ahead, behind = only_ahead(right, 2), only_behind(left, 2)
    even = iota(ahead[0].shape, 1) % 2 == 0
    return [jnp.where(even, a, pltpu.roll(b, 2, 1)) for a, b in zip(ahead, behind)]


def within_plane(q, base, state, products, edge, x_ahead, x_behind):
    rows, lanes = q[0].shape
    row, lane = iota((rows, lanes), 0), iota((rows, lanes), 1)
    y = flux_of(q, state, 2, products)
    x = flux_of(q, state, 1, products)
    y_a, y_b, x_a, x_b = ahead_of(base, y), behind_of(base, y), ahead_of(base, x), behind_of(base, x)
    sums = []
    for f in range(len(q)):
        part = jnp.where(lane == lanes - 1, edge[f], pltpu.roll(y_a[f], lanes - 1, 1))
        part = part + jnp.where(lane == 0, edge[f], pltpu.roll(y_b[f], 1, 1))
        other = jnp.where(row == rows - 1, x_ahead[f], pltpu.roll(x_a[f], rows - 1, 0))
        other = other + jnp.where(row == 0, x_behind[f], pltpu.roll(x_b[f], 1, 0))
        sums.append(part + other)
    return sums


def advanced(start, now, total):
    return 0.75 * start + (0.25 * (1.0 - 6.0 * VISCOUS * TIME_STEP)) * now + (0.125 * TIME_STEP) * total


def stencil_body(first, *refs):
    now_ref, start_ref, y_a_ref, y_b_ref, x_a_ref, x_b_ref = refs[:6]
    next_ref, halo_ref = refs[-2:]
    fields, chunk, _, lanes = next_ref.shape
    planes = now_ref.shape[1]
    step = pl.program_id(0)
    base = (first + step) * chunk
    span = range(fields)

    @pl.when(step == 0)
    def _():
        packed = y_halo([y_a_ref[f] for f in span], [y_b_ref[f] for f in span])
        for f in span:
            halo_ref[f] = packed[f]

    lines = pl.ds(pl.multiple_of(base, 8), chunk)
    x_lo, x_hi = sides("gx", [x_a_ref[f, lines, :] for f in span], [x_b_ref[f, lines, :] for f in span])
    x_behind = only_behind(x_lo, 1)
    x_ahead = only_ahead(x_hi, 1)
    turn = lax.rem(lanes - 2 * base, lanes)
    halo = [pltpu.roll(halo_ref[f], turn, 1) for f in span]
    z = jnp.maximum(base - 1, 0)
    before = only_behind([now_ref[f, z] for f in span], 3)
    pending = None

    def finish(j, ahead):
        for f in span:
            total = pending[f] + ahead[f]
            next_ref[f, j] = advanced(start_ref[f, base + j], now_ref[f, base + j], total)

    for j in range(chunk):
        q = [now_ref[f, base + j] for f in span]
        state = state_of(q)
        products = products_of(q, state)
        half = scaled(q)
        flux = flux_of(q, state, 3, products)
        if pending is not None:
            finish(j - 1, ahead_of(half, flux))
        edge = [pltpu.roll(halo[f], lanes - 1 - 2 * j, 1) for f in span]
        sums = within_plane(
            q, half, state, products, edge,
            [x_ahead[f][j : j + 1] for f in span], [x_behind[f][j : j + 1] for f in span],
        )
        pending = [sums[f] + before[f] for f in span]
        before = behind_of(half, flux)
    z = jnp.minimum(base + chunk, planes - 1)
    finish(chunk - 1, only_ahead([now_ref[f, z] for f in span], 3))


def stencil(now, start, around, first, count, into):
    fields, _, rows, lanes = now.shape
    chunk = CHUNK
    specs = [IN_VMEM] * 6
    operands = [now, start, *around]
    if into is not None:
        specs.append(pl.BlockSpec(memory_space=pl.ANY))
        operands.append(into)
    return pl.pallas_call(
        functools.partial(stencil_body, first),
        out_shape=jax.ShapeDtypeStruct(now.shape, now.dtype),
        grid=(count,),
        in_specs=specs,
        out_specs=pl.BlockSpec((fields, chunk, rows, lanes), lambda c: (0, first + c, 0, 0)),
        scratch_shapes=[pltpu.VMEM((fields, rows, lanes), jnp.float32)],
        input_output_aliases={} if into is None else {len(operands) - 1: 0},
        compiler_params=ROOM,
    )(*operands)


def relayout_body(older_ref, out_ref, *cells_refs):
    older, pair, rows, lanes = older_ref.shape
    snaps = out_ref.shape[1]
    base = pl.program_id(0) * pair

    @pl.when(pl.program_id(0) == 0)
    def _():
        for ref in cells_refs:
            ref[pl.ds(older * rows, (snaps - older) * rows), :] = jnp.zeros(
                ((snaps - older) * rows, lanes), jnp.float32
            )

    for which, ref in enumerate(cells_refs):
        ref[pl.ds(0, older * rows), :] = older_ref[:, which].astype(jnp.float32).reshape(older * rows, lanes)
    for which, ref in enumerate(cells_refs):
        for r in range(rows):
            part = ref[pl.ds(r, snaps, stride=rows), :]
            out_ref[base + which, :, r * lanes : (r + 1) * lanes] = part.astype(out_ref.dtype)


def relayout(history):
    older, samples, rows, lanes = history.shape
    snaps = older + 1
    pair = 2
    return pl.pallas_call(
        relayout_body,
        out_shape=jax.ShapeDtypeStruct((samples, snaps, rows * lanes), history.dtype),
        grid=(samples // pair,),
        in_specs=[pl.BlockSpec((older, pair, rows, lanes), lambda p: (0, p, 0, 0))],
        out_specs=IN_VMEM,
        scratch_shapes=[pltpu.VMEM((snaps * rows, lanes), jnp.float32)] * pair,
        compiler_params=ROOM,
        name="relayout",
    )(history)


def gram_body(
    cells_ref, now_ref, start_ref, y_a_ref, y_b_ref, x_a_ref, x_b_ref,
    mine_ref, sent_ref, newest_ref, total_ref, halo_ref, folded_ref, *, axis,
):
    snaps, width = cells_ref.shape[1:]
    pair = newest_ref.shape[0]
    fields, rows, lanes = halo_ref.shape
    step = pl.program_id(0)
    base = pair * jnp.maximum(step - 1, 0)
    groups = pl.num_programs(0) - 1
    span = range(fields)
    tile = 16

    @pl.when(step == 0)
    def _():
        newest_ref[...] = jnp.zeros_like(newest_ref)
        packed = y_halo([y_a_ref[f] for f in span], [y_b_ref[f] for f in span])
        for f in span:
            halo_ref[f] = packed[f]

    bottom = iota((tile, width), 0) == tile - 1
    parts = []
    for which in range(pair):
        row = jnp.concatenate([newest_ref[which, r : r + 1, :] for r in range(rows)], axis=1)
        last = cells_ref[base + which, snaps - tile :, :].astype(jnp.float32)
        last = jnp.where(bottom, row, last).astype(cells_ref.dtype)
        parts.append(jnp.concatenate([cells_ref[base + which, : snaps - tile, :], last], axis=0))
    matrix = jnp.concatenate(parts, axis=1)
    product = lax.dot_general(
        matrix, matrix, (((1,), (1,)), ((), ())), preferred_element_type=jnp.float32
    )

    def newest(which):
        z = ZSUB * (pair * jnp.minimum(step, groups - 1) + which)
        q = [now_ref[f, z] for f in span]
        state = state_of(q)
        products = products_of(q, state)
        half = scaled(q)
        turn = lax.rem(2 * lanes - 1 - 2 * z, lanes)
        edge = [pltpu.roll(halo_ref[f], turn, 1) for f in span]
        x_lo, x_hi = sides(
            "gx", [x_a_ref[f, pl.ds(z, 1), :] for f in span], [x_b_ref[f, pl.ds(z, 1), :] for f in span]
        )
        x_behind, x_ahead = only_behind(x_lo, 1), only_ahead(x_hi, 1)
        sums = within_plane(q, half, state, products, edge, x_ahead, x_behind)
        low = jnp.maximum(z - 1, 0)
        before = only_behind([now_ref[f, low] for f in span], 3)
        after = only_ahead([now_ref[f, z + 1] for f in span], 3)
        out = [advanced(start_ref[f, z], q[f], sums[f] + before[f] + after[f]) for f in span]
        return state_of(out)[1]

    fresh = [newest(which) for which in range(pair)]
    for which in range(pair):
        newest_ref[which] = fresh[which]
    total_ref[...] = jnp.where(step > 1, total_ref[...], 0.0) + product

    @pl.when(step == groups)
    def _():
        half = snaps // 2
        first, final = total_ref[:half, :half], total_ref[half:, half:]
        r, c = iota((half, half), 0), iota((half, half), 1)
        folded_ref[:half] = jnp.where(r <= c, first, final)
        folded_ref[half : 2 * half] = total_ref[:half, half:]
        diagonal = jnp.sum(jnp.where(r == c, final, 0.0), axis=0, keepdims=True)
        folded_ref[2 * half :] = jnp.broadcast_to(diagonal, (folded_ref.shape[0] - 2 * half, half))
        size = mine_ref.shape[0]
        side = lax.rem(lax.axis_index(axis), 2)
        mine_ref[...] = folded_ref[pl.ds(pl.multiple_of(side * size, 8), size), :]
        sent_ref[...] = folded_ref[pl.ds(pl.multiple_of((1 - side) * size, 8), size), :]


def gram(cells, now, start, around, axis):
    samples, snaps, _ = cells.shape
    fields, _, rows, lanes = now.shape
    half = snaps // 2
    pair = 2
    groups = samples // pair
    size = half + 8
    return pl.pallas_call(
        functools.partial(gram_body, axis=axis),
        out_shape=(jax.ShapeDtypeStruct((size, half), jnp.float32),) * 2,
        grid=(groups + 1,),
        in_specs=[IN_VMEM] * 7,
        out_specs=(IN_VMEM, IN_VMEM),
        scratch_shapes=[
            pltpu.VMEM((pair, rows, lanes), jnp.float32),
            pltpu.VMEM((snaps, snaps), jnp.float32),
            pltpu.VMEM((fields, rows, lanes), jnp.float32),
            pltpu.VMEM((2 * size, half), jnp.float32),
        ],
        compiler_params=ROOM,
        name="gram",
    )(cells, now, start, *around)


def factor_body(scale, axis, mine_ref, other_ref, out_ref, gram_ref, folded_ref):
    size, half = mine_ref.shape
    side = lax.rem(lax.axis_index(axis), 2)
    folded_ref[pl.ds(pl.multiple_of(side * size, 8), size), :] = mine_ref[...]
    folded_ref[pl.ds(pl.multiple_of((1 - side) * size, 8), size), :] = other_ref[...]
    group = 8
    r, c = iota((half, half), 0), iota((half, half), 1)
    mixed = folded_ref[:half] * scale
    turned = mixed.T
    gram_ref[:half, :half] = jnp.where(r <= c, mixed, turned)
    gram_ref[:half, half:] = folded_ref[half : 2 * half] * scale
    diagonal = jnp.broadcast_to(folded_ref[2 * half : 2 * half + 1] * scale, (half, half))
    gram_ref[half:, half:] = jnp.where(r == c, diagonal, jnp.where(r > c, mixed, turned))
    out_ref[half:, :half] = jnp.zeros((half, half), jnp.float32)
    sub, lane = iota((group, half), 0), iota((group, half), 1)
    span = range(group)

    def column(x, index):
        return jnp.broadcast_to(x[:, index : index + 1], (group, half))

    def line(x, index):
        return jnp.broadcast_to(x[index : index + 1, :], (group, half))

    per = half // group
    for panel in range(2):
        width = 2 - panel
        tiles = [
            [
                gram_ref[pl.ds(panel * half + group * t, group), pl.ds((panel + v) * half, half)]
                for v in range(width)
            ]
            for t in range(per)
        ]
        for t in range(per):
            first = group * t
            own = [column(tiles[t][0], first + j) for j in span]
            pivot = {(i, j): line(own[j], i) for j in span for i in range(j + 1)}
            rows = [[line(x, i) for x in tiles[t]] for i in span]
            later = range(t + 1, per)
            lower = {m: [column(tiles[m][0], first + j) for j in span] for m in later}
            for i in span:
                inverse = lax.rsqrt(pivot[i, i])
                for j in range(i + 1, group):
                    pivot[i, j] = pivot[i, j] * inverse
                for j in range(i + 1, group):
                    for k in range(j, group):
                        pivot[j, k] = pivot[j, k] - pivot[i, j] * pivot[i, k]
                rows[i] = [x * inverse for x in rows[i]]
                for j in range(i + 1, group):
                    rows[j] = [a - pivot[i, j] * b for a, b in zip(rows[j], rows[i])]
                for m in later:
                    entry = lower[m][i] * inverse
                    for j in range(i + 1, group):
                        lower[m][j] = lower[m][j] - entry * pivot[i, j]
                    tiles[m] = [a - entry * b for a, b in zip(tiles[m], rows[i])]
            for v in range(width):
                merged = rows[0][v]
                for i in range(1, group):
                    merged = jnp.where(sub == i, rows[i][v], merged)
                if v == 0:
                    merged = jnp.where(lane >= first + sub, merged, 0.0)
                out_ref[pl.ds(panel * half + first, group), pl.ds((panel + v) * half, half)] = merged
        if panel == 0:
            across = out_ref[:half, half:]
            gram_ref[half:, half:] = gram_ref[half:, half:] - lax.dot_general(
                across,
                across,
                (((0,), (0,)), ((), ())),
                precision=lax.Precision.HIGHEST,
                preferred_element_type=jnp.float32,
            )


def factor(mine, other, rows_total, axis):
    size, half = mine.shape
    return pl.pallas_call(
        functools.partial(factor_body, 1.0 / rows_total, axis),
        out_shape=jax.ShapeDtypeStruct((2 * half, 2 * half), jnp.float32),
        in_specs=[IN_VMEM, IN_VMEM],
        out_specs=IN_VMEM,
        scratch_shapes=[
            pltpu.VMEM((2 * half, 2 * half), jnp.float32),
            pltpu.VMEM((2 * size, half), jnp.float32),
        ],
        compiler_params=ROOM,
        name="factor",
    )(mine, other)


def local(section_start, section_now, history):
    axes = ("gx", "gy")
    count = lax.axis_size("gx") * lax.axis_size("gy")
    first, second, cols = edges(section_now)

    def neighbours(part, axis, by):
        size = lax.axis_size(axis)
        assert size % 2 == 0
        return lax.ppermute(part, axis, [(i, (i + by * (-1) ** i) % size) for i in range(size)])

    def swap(part, bit):
        return lax.ppermute(part, axes, [(i, i ^ bit) for i in range(count)])

    x_a, x_b = neighbours(first, "gx", 1), neighbours(second, "gx", -1)
    y_a, y_b = neighbours(cols, "gy", 1), neighbours(cols, "gy", -1)
    around = (y_a, y_b, x_a, x_b)
    cells = relayout(pltpu.with_memory_space_constraint(history, pltpu.HBM))
    mine, sent = gram(cells, section_now, section_start, around, "gy")
    mine = mine + swap(sent, 1)
    bit = 2
    while bit < count:
        mine = mine + swap(mine, bit)
        bit *= 2
    rows_total = history[0].size * count
    triangle = factor(mine, swap(mine, 1), rows_total, "gy")
    chunks = section_now.shape[1] // CHUNK
    section_next = None
    for piece in range(PIECES):
        low, high = piece * chunks // PIECES, (piece + 1) * chunks // PIECES
        section_next = stencil(section_now, section_start, around, low, high - low, section_next)
    return (section_next, triangle)


def solution(mesh):
    placed = P(None, None, "gx", "gy")
    return jax.shard_map(
        local,
        mesh=mesh,
        in_specs=(placed, placed, placed),
        out_specs=(placed, P()),
        check_vma=False,
    )
```

```python
import functools

import jax
import jax.numpy as jnp
from jax import lax
from jax.experimental import pallas as pl
from jax.experimental.pallas import tpu as pltpu
from jax.sharding import PartitionSpec as P


ZSUB = 4
GAMMA_LESS = 0.4
TIME_STEP = 0.2
VISCOUS = 0.25
CHUNK = 8
PIECES = 4
IN_VMEM = pl.BlockSpec(memory_space=pltpu.VMEM)
ROOM = pltpu.CompilerParams(vmem_limit_bytes=20 * 1024 * 1024)


def iota(shape, dim):
    return lax.broadcasted_iota(jnp.int32, shape, dim)


def is_even(axis):
    return lax.rem(lax.axis_index(axis), 2) == 0


def edges_body(now_ref, first_ref, second_ref, cols_ref):
    fields, planes, rows, lanes = now_ref.shape
    even = is_even("gx")
    lo, hi = now_ref[:, :, 0, :], now_ref[:, :, rows - 1, :]
    first_ref[...] = jnp.where(even, hi, lo)
    second_ref[...] = jnp.where(even, lo, hi)
    key = lax.rem((iota((rows, lanes), 1) + 1) // 2, planes)
    masks = 8
    for f in range(fields):
        parts = [jnp.zeros((rows, lanes), jnp.float32)] * masks
        for z in range(planes):
            cells = now_ref[f, z]
            rolled = pltpu.roll(cells, 2 * z, 1) if z else cells
            parts[z % masks] = jnp.where(key == z, rolled, parts[z % masks])
        while len(parts) > 1:
            parts = [x + y for x, y in zip(parts[::2], parts[1::2])]
        cols_ref[f] = parts[0]


def edges(now):
    fields, planes, rows, lanes = now.shape
    assert 2 * planes == lanes
    line = jax.ShapeDtypeStruct((fields, planes, lanes), now.dtype)
    return pl.pallas_call(
        edges_body,
        out_shape=(line, line, jax.ShapeDtypeStruct((fields, rows, lanes), now.dtype)),
        in_specs=[IN_VMEM],
        out_specs=(IN_VMEM, IN_VMEM, IN_VMEM),
        compiler_params=ROOM,
        name="edges",
    )(now)


def state_of(q):
    inverse = 1.0 / q[0]
    speed = [q[k] * inverse for k in (1, 2, 3)]
    twice = q[1] * speed[0] + q[2] * speed[1] + q[3] * speed[2]
    return speed, GAMMA_LESS * (q[4] - 0.5 * twice)


def products_of(q, state):
    speed, pressure = state
    total = q[4] + pressure
    shared = {}
    for i in range(3):
        for j in range(i, 3):
            shared[i, j] = q[1 + i] * speed[j]
    return shared, total


def flux_of(q, state, direction, products=None):
    speed, pressure = state
    shared, total = products or products_of(q, state)
    d = direction - 1
    columns = [q[direction]] + [shared[min(i, d), max(i, d)] for i in range(3)] + [total * speed[d]]
    columns[direction] = columns[direction] + pressure
    return columns


def scaled(q):
    return [2.0 * VISCOUS * x for x in q]


def ahead_of(base, flux):
    return [a - b for a, b in zip(base, flux)]


def behind_of(base, flux):
    return [a + b for a, b in zip(base, flux)]


def only_ahead(q, direction):
    return ahead_of(scaled(q), flux_of(q, state_of(q), direction))


def only_behind(q, direction):
    return behind_of(scaled(q), flux_of(q, state_of(q), direction))


def sides(axis, first, second):
    even = is_even(axis)
    below = [jnp.where(even, b, a) for a, b in zip(first, second)]
    above = [jnp.where(even, a, b) for a, b in zip(first, second)]
    return below, above


def y_halo(first, second):
    left, right = sides("gy", first, second)
    ahead, behind = only_ahead(right, 2), only_behind(left, 2)
    even = iota(ahead[0].shape, 1) % 2 == 0
    return [jnp.where(even, a, pltpu.roll(b, 2, 1)) for a, b in zip(ahead, behind)]


def within_plane(q, base, state, products, edge, x_ahead, x_behind):
    rows, lanes = q[0].shape
    row, lane = iota((rows, lanes), 0), iota((rows, lanes), 1)
    y = flux_of(q, state, 2, products)
    x = flux_of(q, state, 1, products)
    y_a, y_b, x_a, x_b = ahead_of(base, y), behind_of(base, y), ahead_of(base, x), behind_of(base, x)
    sums = []
    for f in range(len(q)):
        part = jnp.where(lane == lanes - 1, edge[f], pltpu.roll(y_a[f], lanes - 1, 1))
        part = part + jnp.where(lane == 0, edge[f], pltpu.roll(y_b[f], 1, 1))
        other = jnp.where(row == rows - 1, x_ahead[f], pltpu.roll(x_a[f], rows - 1, 0))
        other = other + jnp.where(row == 0, x_behind[f], pltpu.roll(x_b[f], 1, 0))
        sums.append(part + other)
    return sums


def advanced(start, now, total):
    return 0.75 * start + (0.25 * (1.0 - 6.0 * VISCOUS * TIME_STEP)) * now + (0.125 * TIME_STEP) * total


def stencil_body(first, *refs):
    now_ref, start_ref, y_a_ref, y_b_ref, x_a_ref, x_b_ref = refs[:6]
    next_ref, halo_ref = refs[-2:]
    fields, chunk, _, lanes = next_ref.shape
    planes = now_ref.shape[1]
    step = pl.program_id(0)
    base = (first + step) * chunk
    span = range(fields)

    @pl.when(step == 0)
    def _():
        packed = y_halo([y_a_ref[f] for f in span], [y_b_ref[f] for f in span])
        for f in span:
            halo_ref[f] = packed[f]

    lines = pl.ds(pl.multiple_of(base, 8), chunk)
    x_lo, x_hi = sides("gx", [x_a_ref[f, lines, :] for f in span], [x_b_ref[f, lines, :] for f in span])
    x_behind = only_behind(x_lo, 1)
    x_ahead = only_ahead(x_hi, 1)
    turn = lax.rem(lanes - 2 * base, lanes)
    halo = [pltpu.roll(halo_ref[f], turn, 1) for f in span]
    z = jnp.maximum(base - 1, 0)
    before = only_behind([now_ref[f, z] for f in span], 3)
    pending = None

    def finish(j, ahead):
        for f in span:
            total = pending[f] + ahead[f]
            next_ref[f, j] = advanced(start_ref[f, base + j], now_ref[f, base + j], total)

    for j in range(chunk):
        q = [now_ref[f, base + j] for f in span]
        state = state_of(q)
        products = products_of(q, state)
        half = scaled(q)
        flux = flux_of(q, state, 3, products)
        if pending is not None:
            finish(j - 1, ahead_of(half, flux))
        edge = [pltpu.roll(halo[f], lanes - 1 - 2 * j, 1) for f in span]
        sums = within_plane(
            q, half, state, products, edge,
            [x_ahead[f][j : j + 1] for f in span], [x_behind[f][j : j + 1] for f in span],
        )
        pending = [sums[f] + before[f] for f in span]
        before = behind_of(half, flux)
    z = jnp.minimum(base + chunk, planes - 1)
    finish(chunk - 1, only_ahead([now_ref[f, z] for f in span], 3))


def stencil(now, start, around, first, count, into):
    fields, _, rows, lanes = now.shape
    chunk = CHUNK
    specs = [IN_VMEM] * 6
    operands = [now, start, *around]
    if into is not None:
        specs.append(pl.BlockSpec(memory_space=pl.ANY))
        operands.append(into)
    return pl.pallas_call(
        functools.partial(stencil_body, first),
        out_shape=jax.ShapeDtypeStruct(now.shape, now.dtype),
        grid=(count,),
        in_specs=specs,
        out_specs=pl.BlockSpec((fields, chunk, rows, lanes), lambda c: (0, first + c, 0, 0)),
        scratch_shapes=[pltpu.VMEM((fields, rows, lanes), jnp.float32)],
        input_output_aliases={} if into is None else {len(operands) - 1: 0},
        compiler_params=ROOM,
    )(*operands)


def relayout_body(older_ref, out_ref, *cells_refs):
    older, group, rows, lanes = older_ref.shape
    snaps = out_ref.shape[1]
    base = pl.program_id(0) * group
    stride = rows + 1

    @pl.when(pl.program_id(0) == 0)
    def _():
        for ref in cells_refs:
            for snap in range(older, snaps):
                ref[pl.ds(snap * stride, rows), :] = jnp.zeros((rows, lanes), jnp.float32)

    for which, ref in enumerate(cells_refs):
        for snap in range(older):
            ref[pl.ds(snap * stride, rows), :] = older_ref[snap, which].astype(jnp.float32)
    for which, ref in enumerate(cells_refs):
        for r in range(rows):
            part = ref[pl.ds(r, snaps, stride=stride), :]
            out_ref[base + which, :, r * lanes : (r + 1) * lanes] = part.astype(out_ref.dtype)


def relayout(history):
    older, samples, rows, lanes = history.shape
    snaps = older + 1
    group = 4
    return pl.pallas_call(
        relayout_body,
        out_shape=jax.ShapeDtypeStruct((samples, snaps, rows * lanes), history.dtype),
        grid=(samples // group,),
        in_specs=[pl.BlockSpec((older, group, rows, lanes), lambda p: (0, p, 0, 0))],
        out_specs=IN_VMEM,
        scratch_shapes=[pltpu.VMEM((snaps * (rows + 1), lanes), jnp.float32)] * group,
        compiler_params=ROOM,
        name="relayout",
    )(history)


def gram_body(
    cells_ref, now_ref, start_ref, y_a_ref, y_b_ref, x_a_ref, x_b_ref,
    mine_ref, sent_ref, newest_ref, total_ref, halo_ref, folded_ref, *, axis,
):
    snaps, width = cells_ref.shape[1:]
    pair = newest_ref.shape[0]
    fields, rows, lanes = halo_ref.shape
    step = pl.program_id(0)
    base = pair * jnp.maximum(step - 1, 0)
    groups = pl.num_programs(0) - 1
    span = range(fields)
    tile = 16

    @pl.when(step == 0)
    def _():
        newest_ref[...] = jnp.zeros_like(newest_ref)
        packed = y_halo([y_a_ref[f] for f in span], [y_b_ref[f] for f in span])
        for f in span:
            halo_ref[f] = packed[f]

    bottom = iota((tile, width), 0) == tile - 1
    parts = []
    for which in range(pair):
        row = jnp.concatenate([newest_ref[which, r : r + 1, :] for r in range(rows)], axis=1)
        last = cells_ref[base + which, snaps - tile :, :].astype(jnp.float32)
        last = jnp.where(bottom, row, last).astype(cells_ref.dtype)
        parts.append(jnp.concatenate([cells_ref[base + which, : snaps - tile, :], last], axis=0))
    matrix = jnp.concatenate(parts, axis=1)
    product = lax.dot_general(
        matrix, matrix, (((1,), (1,)), ((), ())), preferred_element_type=jnp.float32
    )

    def newest(which):
        z = ZSUB * (pair * jnp.minimum(step, groups - 1) + which)
        q = [now_ref[f, z] for f in span]
        state = state_of(q)
        products = products_of(q, state)
        half = scaled(q)
        turn = lax.rem(2 * lanes - 1 - 2 * z, lanes)
        edge = [pltpu.roll(halo_ref[f], turn, 1) for f in span]
        x_lo, x_hi = sides(
            "gx", [x_a_ref[f, pl.ds(z, 1), :] for f in span], [x_b_ref[f, pl.ds(z, 1), :] for f in span]
        )
        x_behind, x_ahead = only_behind(x_lo, 1), only_ahead(x_hi, 1)
        sums = within_plane(q, half, state, products, edge, x_ahead, x_behind)
        low = jnp.maximum(z - 1, 0)
        before = only_behind([now_ref[f, low] for f in span], 3)
        after = only_ahead([now_ref[f, z + 1] for f in span], 3)
        out = [advanced(start_ref[f, z], q[f], sums[f] + before[f] + after[f]) for f in span]
        return state_of(out)[1]

    fresh = [newest(which) for which in range(pair)]
    for which in range(pair):
        newest_ref[which] = fresh[which]
    total_ref[...] = jnp.where(step > 1, total_ref[...], 0.0) + product

    @pl.when(step == groups)
    def _():
        half = snaps // 2
        first, final = total_ref[:half, :half], total_ref[half:, half:]
        r, c = iota((half, half), 0), iota((half, half), 1)
        folded_ref[:half] = jnp.where(r <= c, first, final)
        folded_ref[half : 2 * half] = total_ref[:half, half:]
        diagonal = jnp.sum(jnp.where(r == c, final, 0.0), axis=0, keepdims=True)
        folded_ref[2 * half :] = jnp.broadcast_to(diagonal, (folded_ref.shape[0] - 2 * half, half))
        size = mine_ref.shape[0]
        side = lax.rem(lax.axis_index(axis), 2)
        mine_ref[...] = folded_ref[pl.ds(pl.multiple_of(side * size, 8), size), :]
        sent_ref[...] = folded_ref[pl.ds(pl.multiple_of((1 - side) * size, 8), size), :]


def gram(cells, now, start, around, axis):
    samples, snaps, _ = cells.shape
    fields, _, rows, lanes = now.shape
    half = snaps // 2
    pair = 2
    groups = samples // pair
    size = half + 16
    return pl.pallas_call(
        functools.partial(gram_body, axis=axis),
        out_shape=(jax.ShapeDtypeStruct((size, half), jnp.float32),) * 2,
        grid=(groups + 1,),
        in_specs=[IN_VMEM] * 7,
        out_specs=(IN_VMEM, IN_VMEM),
        scratch_shapes=[
            pltpu.VMEM((pair, rows, lanes), jnp.float32),
            pltpu.VMEM((snaps, snaps), jnp.float32),
            pltpu.VMEM((fields, rows, lanes), jnp.float32),
            pltpu.VMEM((2 * size, half), jnp.float32),
        ],
        compiler_params=ROOM,
        name="gram",
    )(cells, now, start, *around)


def factor_body(scale, axis, mine_ref, other_ref, out_ref, gram_ref, folded_ref):
    size, half = mine_ref.shape
    side = lax.rem(lax.axis_index(axis), 2)
    folded_ref[pl.ds(pl.multiple_of(side * size, 8), size), :] = mine_ref[...]
    folded_ref[pl.ds(pl.multiple_of((1 - side) * size, 8), size), :] = other_ref[...]
    group = 8
    r, c = iota((half, half), 0), iota((half, half), 1)
    mixed = folded_ref[:half] * scale
    turned = mixed.T
    gram_ref[:half, :half] = jnp.where(r <= c, mixed, turned)
    gram_ref[:half, half:] = folded_ref[half : 2 * half] * scale
    diagonal = jnp.broadcast_to(folded_ref[2 * half : 2 * half + 1] * scale, (half, half))
    gram_ref[half:, half:] = jnp.where(r == c, diagonal, jnp.where(r > c, mixed, turned))
    out_ref[half:, :half] = jnp.zeros((half, half), jnp.float32)
    sub, lane = iota((group, half), 0), iota((group, half), 1)
    span = range(group)

    def column(x, index):
        return jnp.broadcast_to(x[:, index : index + 1], (group, half))

    def line(x, index):
        return jnp.broadcast_to(x[index : index + 1, :], (group, half))

    per = half // group
    for panel in range(2):
        width = 2 - panel
        tiles = [
            [
                gram_ref[pl.ds(panel * half + group * t, group), pl.ds((panel + v) * half, half)]
                for v in range(width)
            ]
            for t in range(per)
        ]
        for t in range(per):
            first = group * t
            own = [column(tiles[t][0], first + j) for j in span]
            pivot = {(i, j): line(own[j], i) for j in span for i in range(j + 1)}
            rows = [[line(x, i) for x in tiles[t]] for i in span]
            later = range(t + 1, per)
            lower = {m: [column(tiles[m][0], first + j) for j in span] for m in later}
            for i in span:
                inverse = lax.rsqrt(pivot[i, i])
                for j in range(i + 1, group):
                    pivot[i, j] = pivot[i, j] * inverse
                for j in range(i + 1, group):
                    for k in range(j, group):
                        pivot[j, k] = pivot[j, k] - pivot[i, j] * pivot[i, k]
                rows[i] = [x * inverse for x in rows[i]]
                for j in range(i + 1, group):
                    rows[j] = [a - pivot[i, j] * b for a, b in zip(rows[j], rows[i])]
                for m in later:
                    entry = lower[m][i] * inverse
                    for j in range(i + 1, group):
                        lower[m][j] = lower[m][j] - entry * pivot[i, j]
                    tiles[m] = [a - entry * b for a, b in zip(tiles[m], rows[i])]
            for v in range(width):
                merged = rows[0][v]
                for i in range(1, group):
                    merged = jnp.where(sub == i, rows[i][v], merged)
                if v == 0:
                    merged = jnp.where(lane >= first + sub, merged, 0.0)
                out_ref[pl.ds(panel * half + first, group), pl.ds((panel + v) * half, half)] = merged
        if panel == 0:
            across = out_ref[:half, half:]
            gram_ref[half:, half:] = gram_ref[half:, half:] - lax.dot_general(
                across,
                across,
                (((0,), (0,)), ((), ())),
                precision=lax.Precision.HIGHEST,
                preferred_element_type=jnp.float32,
            )


def factor(mine, other, rows_total, axis):
    size, half = mine.shape
    return pl.pallas_call(
        functools.partial(factor_body, 1.0 / rows_total, axis),
        out_shape=jax.ShapeDtypeStruct((2 * half, 2 * half), jnp.float32),
        in_specs=[IN_VMEM, IN_VMEM],
        out_specs=IN_VMEM,
        scratch_shapes=[
            pltpu.VMEM((2 * half, 2 * half), jnp.float32),
            pltpu.VMEM((2 * size, half), jnp.float32),
        ],
        compiler_params=ROOM,
        name="factor",
    )(mine, other)


def local(section_start, section_now, history):
    axes = ("gx", "gy")
    count = lax.axis_size("gx") * lax.axis_size("gy")
    first, second, cols = edges(section_now)

    def neighbours(part, axis, by):
        size = lax.axis_size(axis)
        assert size % 2 == 0
        return lax.ppermute(part, axis, [(i, (i + by * (-1) ** i) % size) for i in range(size)])

    def swap(part, bit):
        return lax.ppermute(part, axes, [(i, i ^ bit) for i in range(count)])

    x_a, x_b = neighbours(first, "gx", 1), neighbours(second, "gx", -1)
    y_a, y_b = neighbours(cols, "gy", 1), neighbours(cols, "gy", -1)
    around = (y_a, y_b, x_a, x_b)
    cells = relayout(pltpu.with_memory_space_constraint(history, pltpu.HBM))
    mine, sent = gram(cells, section_now, section_start, around, "gy")
    whole = mine + swap(sent, 1)
    low = (lax.axis_index("gy") & 2) == 0
    quarter = whole.shape[0] // 2
    top, bottom = whole[:quarter], whole[quarter:]
    part = jnp.where(low, top, bottom) + swap(jnp.where(low, bottom, top), 2)
    bit = 4
    while bit < count:
        part = part + swap(part, bit)
        bit *= 2
    other = swap(part, 2)
    whole = jnp.concatenate([jnp.where(low, part, other), jnp.where(low, other, part)])
    rows_total = history[0].size * count
    other = swap(whole, 1)
    triangle = factor(whole, other, rows_total, "gy")
    chunks = section_now.shape[1] // CHUNK
    section_next = None
    for piece in range(PIECES):
        low, high = piece * chunks // PIECES, (piece + 1) * chunks // PIECES
        section_next = stencil(section_now, section_start, around, low, high - low, section_next)
    return (section_next, triangle)


def solution(mesh):
    placed = P(None, None, "gx", "gy")
    return jax.shard_map(
        local,
        mesh=mesh,
        in_specs=(placed, placed, placed),
        out_specs=(placed, P()),
        check_vma=False,
    )
```

```python
import functools

import jax
import jax.numpy as jnp
from jax import lax
from jax.experimental import pallas as pl
from jax.experimental.pallas import tpu as pltpu
from jax.sharding import PartitionSpec as P


ZSUB = 4
GAMMA_LESS = 0.4
TIME_STEP = 0.2
VISCOUS = 0.25
CHUNK = 8
PIECES = 4
IN_VMEM = pl.BlockSpec(memory_space=pltpu.VMEM)
ROOM = pltpu.CompilerParams(vmem_limit_bytes=20 * 1024 * 1024)
SPREAD = pltpu.CompilerParams(vmem_limit_bytes=20 * 1024 * 1024)


def iota(shape, dim):
    return lax.broadcasted_iota(jnp.int32, shape, dim)


def is_even(axis):
    return lax.rem(lax.axis_index(axis), 2) == 0


def edges_body(now_ref, first_ref, second_ref, cols_ref):
    fields, planes, rows, lanes = now_ref.shape
    even = is_even("gx")
    lo, hi = now_ref[:, :, 0, :], now_ref[:, :, rows - 1, :]
    first_ref[...] = jnp.where(even, hi, lo)
    second_ref[...] = jnp.where(even, lo, hi)
    key = lax.rem((iota((rows, lanes), 1) + 1) // 2, planes)
    masks = 8
    for f in range(fields):
        parts = [jnp.zeros((rows, lanes), jnp.float32)] * masks
        for z in range(planes):
            cells = now_ref[f, z]
            rolled = pltpu.roll(cells, 2 * z, 1) if z else cells
            parts[z % masks] = jnp.where(key == z, rolled, parts[z % masks])
        while len(parts) > 1:
            parts = [x + y for x, y in zip(parts[::2], parts[1::2])]
        cols_ref[f] = parts[0]


def edges(now):
    fields, planes, rows, lanes = now.shape
    assert 2 * planes == lanes
    line = jax.ShapeDtypeStruct((fields, planes, lanes), now.dtype)
    return pl.pallas_call(
        edges_body,
        out_shape=(line, line, jax.ShapeDtypeStruct((fields, rows, lanes), now.dtype)),
        in_specs=[IN_VMEM],
        out_specs=(IN_VMEM, IN_VMEM, IN_VMEM),
        compiler_params=ROOM,
        name="edges",
    )(now)


def state_of(q):
    inverse = 1.0 / q[0]
    speed = [q[k] * inverse for k in (1, 2, 3)]
    twice = q[1] * speed[0] + q[2] * speed[1] + q[3] * speed[2]
    return speed, GAMMA_LESS * (q[4] - 0.5 * twice)


def products_of(q, state):
    speed, pressure = state
    total = q[4] + pressure
    shared = {}
    for i in range(3):
        for j in range(i, 3):
            shared[i, j] = q[1 + i] * speed[j]
    return shared, total


def flux_of(q, state, direction, products=None):
    speed, pressure = state
    shared, total = products or products_of(q, state)
    d = direction - 1
    columns = [q[direction]] + [shared[min(i, d), max(i, d)] for i in range(3)] + [total * speed[d]]
    columns[direction] = columns[direction] + pressure
    return columns


def scaled(q):
    return [2.0 * VISCOUS * x for x in q]


def ahead_of(base, flux):
    return [a - b for a, b in zip(base, flux)]


def behind_of(base, flux):
    return [a + b for a, b in zip(base, flux)]


def only_ahead(q, direction):
    return ahead_of(scaled(q), flux_of(q, state_of(q), direction))


def only_behind(q, direction):
    return behind_of(scaled(q), flux_of(q, state_of(q), direction))


def sides(axis, first, second):
    even = is_even(axis)
    below = [jnp.where(even, b, a) for a, b in zip(first, second)]
    above = [jnp.where(even, a, b) for a, b in zip(first, second)]
    return below, above


def y_halo(first, second):
    left, right = sides("gy", first, second)
    ahead, behind = only_ahead(right, 2), only_behind(left, 2)
    even = iota(ahead[0].shape, 1) % 2 == 0
    return [jnp.where(even, a, pltpu.roll(b, 2, 1)) for a, b in zip(ahead, behind)]


def within_plane(q, base, state, products, edge, x_ahead, x_behind):
    rows, lanes = q[0].shape
    row, lane = iota((rows, lanes), 0), iota((rows, lanes), 1)
    y = flux_of(q, state, 2, products)
    x = flux_of(q, state, 1, products)
    y_a, y_b, x_a, x_b = ahead_of(base, y), behind_of(base, y), ahead_of(base, x), behind_of(base, x)
    sums = []
    for f in range(len(q)):
        part = jnp.where(lane == lanes - 1, edge[f], pltpu.roll(y_a[f], lanes - 1, 1))
        part = part + jnp.where(lane == 0, edge[f], pltpu.roll(y_b[f], 1, 1))
        other = jnp.where(row == rows - 1, x_ahead[f], pltpu.roll(x_a[f], rows - 1, 0))
        other = other + jnp.where(row == 0, x_behind[f], pltpu.roll(x_b[f], 1, 0))
        sums.append(part + other)
    return sums


def advanced(start, now, total):
    return 0.75 * start + (0.25 * (1.0 - 6.0 * VISCOUS * TIME_STEP)) * now + (0.125 * TIME_STEP) * total


def stencil_body(first, *refs):
    now_ref, start_ref, y_a_ref, y_b_ref, x_a_ref, x_b_ref = refs[:6]
    next_ref, halo_ref = refs[-2:]
    fields, chunk, _, lanes = next_ref.shape
    planes = now_ref.shape[1]
    step = pl.program_id(0)
    base = (first + step) * chunk
    span = range(fields)

    @pl.when(step == 0)
    def _():
        packed = y_halo([y_a_ref[f] for f in span], [y_b_ref[f] for f in span])
        for f in span:
            halo_ref[f] = packed[f]

    lines = pl.ds(pl.multiple_of(base, 8), chunk)
    x_lo, x_hi = sides("gx", [x_a_ref[f, lines, :] for f in span], [x_b_ref[f, lines, :] for f in span])
    x_behind = only_behind(x_lo, 1)
    x_ahead = only_ahead(x_hi, 1)
    turn = lax.rem(lanes - 2 * base, lanes)
    halo = [pltpu.roll(halo_ref[f], turn, 1) for f in span]
    z = jnp.maximum(base - 1, 0)
    before = only_behind([now_ref[f, z] for f in span], 3)
    pending = None

    def finish(j, ahead):
        for f in span:
            total = pending[f] + ahead[f]
            next_ref[f, j] = advanced(start_ref[f, base + j], now_ref[f, base + j], total)

    for j in range(chunk):
        q = [now_ref[f, base + j] for f in span]
        state = state_of(q)
        products = products_of(q, state)
        half = scaled(q)
        flux = flux_of(q, state, 3, products)
        if pending is not None:
            finish(j - 1, ahead_of(half, flux))
        edge = [pltpu.roll(halo[f], lanes - 1 - 2 * j, 1) for f in span]
        sums = within_plane(
            q, half, state, products, edge,
            [x_ahead[f][j : j + 1] for f in span], [x_behind[f][j : j + 1] for f in span],
        )
        pending = [sums[f] + before[f] for f in span]
        before = behind_of(half, flux)
    z = jnp.minimum(base + chunk, planes - 1)
    finish(chunk - 1, only_ahead([now_ref[f, z] for f in span], 3))


def stencil(now, start, around, first, count, into):
    fields, _, rows, lanes = now.shape
    chunk = CHUNK
    specs = [IN_VMEM] * 6
    operands = [now, start, *around]
    if into is not None:
        specs.append(pl.BlockSpec(memory_space=pl.ANY))
        operands.append(into)
    return pl.pallas_call(
        functools.partial(stencil_body, first),
        out_shape=jax.ShapeDtypeStruct(now.shape, now.dtype),
        grid=(count,),
        in_specs=specs,
        out_specs=pl.BlockSpec((fields, chunk, rows, lanes), lambda c: (0, first + c, 0, 0)),
        scratch_shapes=[pltpu.VMEM((fields, rows, lanes), jnp.float32)],
        input_output_aliases={} if into is None else {len(operands) - 1: 0},
        compiler_params=ROOM,
    )(*operands)


def relayout_body(older_ref, out_ref, *cells_refs):
    older, group, rows, lanes = older_ref.shape
    snaps = out_ref.shape[1]
    base = pl.program_id(0) * group
    stride = rows + 1

    @pl.when(pl.program_id(0) == 0)
    def _():
        for ref in cells_refs:
            for snap in range(older, snaps):
                ref[pl.ds(snap * stride, rows), :] = jnp.zeros((rows, lanes), jnp.float32)

    for which, ref in enumerate(cells_refs):
        for snap in range(older):
            ref[pl.ds(snap * stride, rows), :] = older_ref[snap, which].astype(jnp.float32)
    for which, ref in enumerate(cells_refs):
        for r in range(rows):
            part = ref[pl.ds(r, snaps, stride=stride), :]
            out_ref[base + which, :, r * lanes : (r + 1) * lanes] = part.astype(out_ref.dtype)


def relayout(history):
    older, samples, rows, lanes = history.shape
    snaps = older + 1
    group = 4
    return pl.pallas_call(
        relayout_body,
        out_shape=jax.ShapeDtypeStruct((samples, snaps, rows * lanes), history.dtype),
        grid=(samples // group,),
        in_specs=[pl.BlockSpec((older, group, rows, lanes), lambda p: (0, p, 0, 0))],
        out_specs=IN_VMEM,
        scratch_shapes=[pltpu.VMEM((snaps * (rows + 1), lanes), jnp.float32)] * group,
        compiler_params=ROOM,
        name="relayout",
    )(history)


def gram_body(
    cells_ref, now_ref, start_ref, y_a_ref, y_b_ref, x_a_ref, x_b_ref,
    mine_ref, sent_ref, newest_ref, total_ref, halo_ref, folded_ref, *, axis,
):
    snaps, width = cells_ref.shape[1:]
    pair = newest_ref.shape[0]
    fields, rows, lanes = halo_ref.shape
    step = pl.program_id(0)
    base = pair * jnp.maximum(step - 1, 0)
    groups = pl.num_programs(0) - 1
    span = range(fields)
    tile = 16

    @pl.when(step == 0)
    def _():
        newest_ref[...] = jnp.zeros_like(newest_ref)
        packed = y_halo([y_a_ref[f] for f in span], [y_b_ref[f] for f in span])
        for f in span:
            halo_ref[f] = packed[f]

    bottom = iota((tile, width), 0) == tile - 1
    parts = []
    for which in range(pair):
        row = jnp.concatenate([newest_ref[which, r : r + 1, :] for r in range(rows)], axis=1)
        last = cells_ref[base + which, snaps - tile :, :].astype(jnp.float32)
        last = jnp.where(bottom, row, last).astype(cells_ref.dtype)
        parts.append(jnp.concatenate([cells_ref[base + which, : snaps - tile, :], last], axis=0))
    matrix = jnp.concatenate(parts, axis=1)
    product = lax.dot_general(
        matrix, matrix, (((1,), (1,)), ((), ())), preferred_element_type=jnp.float32
    )

    def newest(which):
        z = ZSUB * (pair * jnp.minimum(step, groups - 1) + which)
        q = [now_ref[f, z] for f in span]
        state = state_of(q)
        products = products_of(q, state)
        half = scaled(q)
        turn = lax.rem(2 * lanes - 1 - 2 * z, lanes)
        edge = [pltpu.roll(halo_ref[f], turn, 1) for f in span]
        x_lo, x_hi = sides(
            "gx", [x_a_ref[f, pl.ds(z, 1), :] for f in span], [x_b_ref[f, pl.ds(z, 1), :] for f in span]
        )
        x_behind, x_ahead = only_behind(x_lo, 1), only_ahead(x_hi, 1)
        sums = within_plane(q, half, state, products, edge, x_ahead, x_behind)
        low = jnp.maximum(z - 1, 0)
        before = only_behind([now_ref[f, low] for f in span], 3)
        after = only_ahead([now_ref[f, z + 1] for f in span], 3)
        out = [advanced(start_ref[f, z], q[f], sums[f] + before[f] + after[f]) for f in span]
        return state_of(out)[1]

    fresh = [newest(which) for which in range(pair)]
    for which in range(pair):
        newest_ref[which] = fresh[which]
    total_ref[...] = jnp.where(step > 1, total_ref[...], 0.0) + product

    @pl.when(step == groups)
    def _():
        half = snaps // 2
        first, final = total_ref[:half, :half], total_ref[half:, half:]
        r, c = iota((half, half), 0), iota((half, half), 1)
        folded_ref[:half] = jnp.where(r <= c, first, final)
        folded_ref[half : 2 * half] = total_ref[:half, half:]
        diagonal = jnp.sum(jnp.where(r == c, final, 0.0), axis=0, keepdims=True)
        folded_ref[2 * half :] = jnp.broadcast_to(diagonal, (folded_ref.shape[0] - 2 * half, half))
        size = mine_ref.shape[0]
        side = lax.rem(lax.axis_index(axis), 2)
        mine_ref[...] = folded_ref[pl.ds(pl.multiple_of(side * size, 8), size), :]
        sent_ref[...] = folded_ref[pl.ds(pl.multiple_of((1 - side) * size, 8), size), :]


def gram(cells, now, start, around, axis):
    samples, snaps, _ = cells.shape
    fields, _, rows, lanes = now.shape
    half = snaps // 2
    pair = 2
    groups = samples // pair
    size = half + 8
    return pl.pallas_call(
        functools.partial(gram_body, axis=axis),
        out_shape=(jax.ShapeDtypeStruct((size, half), jnp.float32),) * 2,
        grid=(groups + 1,),
        in_specs=[IN_VMEM] * 7,
        out_specs=(IN_VMEM, IN_VMEM),
        scratch_shapes=[
            pltpu.VMEM((pair, rows, lanes), jnp.float32),
            pltpu.VMEM((snaps, snaps), jnp.float32),
            pltpu.VMEM((fields, rows, lanes), jnp.float32),
            pltpu.VMEM((2 * size, half), jnp.float32),
        ],
        compiler_params=SPREAD,
        name="gram",
    )(cells, now, start, *around)


def factor_body(scale, axis, mine_ref, other_ref, out_ref, gram_ref, folded_ref):
    size, half = mine_ref.shape
    side = lax.rem(lax.axis_index(axis), 2)
    folded_ref[pl.ds(pl.multiple_of(side * size, 8), size), :] = mine_ref[...]
    folded_ref[pl.ds(pl.multiple_of((1 - side) * size, 8), size), :] = other_ref[...]
    group = 8
    r, c = iota((half, half), 0), iota((half, half), 1)
    mixed = folded_ref[:half] * scale
    turned = mixed.T
    gram_ref[:half, :half] = jnp.where(r <= c, mixed, turned)
    gram_ref[:half, half:] = folded_ref[half : 2 * half] * scale
    diagonal = jnp.broadcast_to(folded_ref[2 * half : 2 * half + 1] * scale, (half, half))
    gram_ref[half:, half:] = jnp.where(r == c, diagonal, jnp.where(r > c, mixed, turned))
    out_ref[half:, :half] = jnp.zeros((half, half), jnp.float32)
    sub, lane = iota((group, half), 0), iota((group, half), 1)
    span = range(group)

    def column(x, index):
        return jnp.broadcast_to(x[:, index : index + 1], (group, half))

    def line(x, index):
        return jnp.broadcast_to(x[index : index + 1, :], (group, half))

    per = half // group
    for panel in range(2):
        width = 2 - panel
        tiles = [
            [
                gram_ref[pl.ds(panel * half + group * t, group), pl.ds((panel + v) * half, half)]
                for v in range(width)
            ]
            for t in range(per)
        ]
        for t in range(per):
            first = group * t
            own = [column(tiles[t][0], first + j) for j in span]
            pivot = {(i, j): line(own[j], i) for j in span for i in range(j + 1)}
            rows = [[line(x, i) for x in tiles[t]] for i in span]
            later = range(t + 1, per)
            lower = {m: [column(tiles[m][0], first + j) for j in span] for m in later}
            for i in span:
                inverse = lax.rsqrt(pivot[i, i])
                for j in range(i + 1, group):
                    pivot[i, j] = pivot[i, j] * inverse
                for j in range(i + 1, group):
                    for k in range(j, group):
                        pivot[j, k] = pivot[j, k] - pivot[i, j] * pivot[i, k]
                rows[i] = [x * inverse for x in rows[i]]
                for j in range(i + 1, group):
                    rows[j] = [a - pivot[i, j] * b for a, b in zip(rows[j], rows[i])]
                for m in later:
                    entry = lower[m][i] * inverse
                    for j in range(i + 1, group):
                        lower[m][j] = lower[m][j] - entry * pivot[i, j]
                    tiles[m] = [a - entry * b for a, b in zip(tiles[m], rows[i])]
            for v in range(width):
                merged = rows[0][v]
                for i in range(1, group):
                    merged = jnp.where(sub == i, rows[i][v], merged)
                if v == 0:
                    merged = jnp.where(lane >= first + sub, merged, 0.0)
                out_ref[pl.ds(panel * half + first, group), pl.ds((panel + v) * half, half)] = merged
        if panel == 0:
            across = out_ref[:half, half:]
            gram_ref[half:, half:] = gram_ref[half:, half:] - lax.dot_general(
                across,
                across,
                (((0,), (0,)), ((), ())),
                precision=lax.Precision.HIGHEST,
                preferred_element_type=jnp.float32,
            )


def factor(mine, other, rows_total, axis):
    size, half = mine.shape
    return pl.pallas_call(
        functools.partial(factor_body, 1.0 / rows_total, axis),
        out_shape=jax.ShapeDtypeStruct((2 * half, 2 * half), jnp.float32),
        in_specs=[IN_VMEM, IN_VMEM],
        out_specs=IN_VMEM,
        scratch_shapes=[
            pltpu.VMEM((2 * half, 2 * half), jnp.float32),
            pltpu.VMEM((2 * size, half), jnp.float32),
        ],
        compiler_params=ROOM,
        name="factor",
    )(mine, other)


def rounds(count):
    groups = []
    bit = 2
    while bit < count:
        groups.append((bit, 2 * bit, 3 * bit) if 2 * bit < count else (bit,))
        bit *= 4
    return groups


def local(section_start, section_now, history):
    axes = ("gx", "gy")
    count = lax.axis_size("gx") * lax.axis_size("gy")
    first, second, cols = edges(section_now)

    def neighbours(part, axis, by):
        size = lax.axis_size(axis)
        assert size % 2 == 0
        return lax.ppermute(part, axis, [(i, (i + by * (-1) ** i) % size) for i in range(size)])

    def swap(part, bit):
        return lax.ppermute(part, axes, [(i, i ^ bit) for i in range(count)])

    x_a, x_b = neighbours(first, "gx", 1), neighbours(second, "gx", -1)
    y_a, y_b = neighbours(cols, "gy", 1), neighbours(cols, "gy", -1)
    around = (y_a, y_b, x_a, x_b)
    cells = relayout(pltpu.with_memory_space_constraint(history, pltpu.HBM))
    mine, sent = gram(cells, section_now, section_start, around, "gy")
    part = mine + swap(sent, 1)
    for group in rounds(count):
        came = [swap(part, bits) for bits in group]
        part = part + came[0]
        if len(came) > 1:
            part = part + (came[1] + came[2])
    rows_total = history[0].size * count
    triangle = factor(part, swap(part, 1), rows_total, "gy")
    chunks = section_now.shape[1] // CHUNK
    section_next = None
    for piece in range(PIECES):
        low, high = piece * chunks // PIECES, (piece + 1) * chunks // PIECES
        section_next = stencil(section_now, section_start, around, low, high - low, section_next)
    return (section_next, triangle)


def solution(mesh):
    placed = P(None, None, "gx", "gy")
    return jax.shard_map(
        local,
        mesh=mesh,
        in_specs=(placed, placed, placed),
        out_specs=(placed, P()),
        check_vma=False,
    )
```

```python
import functools

import jax
import jax.numpy as jnp
from jax import lax
from jax.experimental import pallas as pl
from jax.experimental.pallas import tpu as pltpu
from jax.sharding import PartitionSpec as P


ZSUB = 4
GAMMA_LESS = 0.4
TIME_STEP = 0.2
VISCOUS = 0.25
CHUNK = 8
PIECES = 4
IN_VMEM = pl.BlockSpec(memory_space=pltpu.VMEM)
ROOM = pltpu.CompilerParams(vmem_limit_bytes=20 * 1024 * 1024)


def iota(shape, dim):
    return lax.broadcasted_iota(jnp.int32, shape, dim)


def is_even(axis):
    return lax.rem(lax.axis_index(axis), 2) == 0


def edges_body(now_ref, first_ref, second_ref, cols_ref):
    planes, rows, lanes = now_ref.shape
    f = pl.program_id(0)
    even = is_even("gx")
    lo, hi = now_ref[:, 0, :], now_ref[:, rows - 1, :]
    first_ref[f] = jnp.where(even, hi, lo)
    second_ref[f] = jnp.where(even, lo, hi)
    key = lax.rem((iota((rows, lanes), 1) + 1) // 2, planes)
    masks = 8
    parts = [jnp.zeros((rows, lanes), jnp.float32)] * masks
    for z in range(planes):
        cells = now_ref[z]
        rolled = pltpu.roll(cells, 2 * z, 1) if z else cells
        parts[z % masks] = jnp.where(key == z, rolled, parts[z % masks])
    while len(parts) > 1:
        parts = [x + y for x, y in zip(parts[::2], parts[1::2])]
    cols_ref[f] = parts[0]


def edges(now):
    fields, planes, rows, lanes = now.shape
    assert 2 * planes == lanes
    line = jax.ShapeDtypeStruct((fields, planes, lanes), now.dtype)
    return pl.pallas_call(
        edges_body,
        out_shape=(line, line, jax.ShapeDtypeStruct((fields, rows, lanes), now.dtype)),
        grid=(fields,),
        in_specs=[pl.BlockSpec((None, planes, rows, lanes), lambda f: (f, 0, 0, 0))],
        out_specs=(IN_VMEM, IN_VMEM, IN_VMEM),
        compiler_params=ROOM,
        name="edges",
    )(now)


def state_of(q):
    inverse = 1.0 / q[0]
    speed = [q[k] * inverse for k in (1, 2, 3)]
    twice = q[1] * speed[0] + q[2] * speed[1] + q[3] * speed[2]
    return speed, GAMMA_LESS * (q[4] - 0.5 * twice)


def products_of(q, state):
    speed, pressure = state
    total = q[4] + pressure
    shared = {}
    for i in range(3):
        for j in range(i, 3):
            shared[i, j] = q[1 + i] * speed[j]
    return shared, total


def flux_of(q, state, direction, products=None):
    speed, pressure = state
    shared, total = products or products_of(q, state)
    d = direction - 1
    columns = [q[direction]] + [shared[min(i, d), max(i, d)] for i in range(3)] + [total * speed[d]]
    columns[direction] = columns[direction] + pressure
    return columns


def scaled(q):
    return [2.0 * VISCOUS * x for x in q]


def ahead_of(base, flux):
    return [a - b for a, b in zip(base, flux)]


def behind_of(base, flux):
    return [a + b for a, b in zip(base, flux)]


def only_ahead(q, direction):
    return ahead_of(scaled(q), flux_of(q, state_of(q), direction))


def only_behind(q, direction):
    return behind_of(scaled(q), flux_of(q, state_of(q), direction))


def sides(axis, first, second):
    even = is_even(axis)
    below = [jnp.where(even, b, a) for a, b in zip(first, second)]
    above = [jnp.where(even, a, b) for a, b in zip(first, second)]
    return below, above


def y_halo(first, second):
    left, right = sides("gy", first, second)
    ahead, behind = only_ahead(right, 2), only_behind(left, 2)
    even = iota(ahead[0].shape, 1) % 2 == 0
    return [jnp.where(even, a, pltpu.roll(b, 2, 1)) for a, b in zip(ahead, behind)]


def within_plane(q, base, state, products, edge, x_ahead, x_behind):
    rows, lanes = q[0].shape
    row, lane = iota((rows, lanes), 0), iota((rows, lanes), 1)
    y = flux_of(q, state, 2, products)
    x = flux_of(q, state, 1, products)
    y_a, y_b, x_a, x_b = ahead_of(base, y), behind_of(base, y), ahead_of(base, x), behind_of(base, x)
    sums = []
    for f in range(len(q)):
        part = jnp.where(lane == lanes - 1, edge[f], pltpu.roll(y_a[f], lanes - 1, 1))
        part = part + jnp.where(lane == 0, edge[f], pltpu.roll(y_b[f], 1, 1))
        other = jnp.where(row == rows - 1, x_ahead[f], pltpu.roll(x_a[f], rows - 1, 0))
        other = other + jnp.where(row == 0, x_behind[f], pltpu.roll(x_b[f], 1, 0))
        sums.append(part + other)
    return sums


def advanced(start, now, total):
    return 0.75 * start + (0.25 * (1.0 - 6.0 * VISCOUS * TIME_STEP)) * now + (0.125 * TIME_STEP) * total


def stencil_body(first, *refs):
    now_ref, start_ref, y_a_ref, y_b_ref, x_a_ref, x_b_ref = refs[:6]
    next_ref, halo_ref = refs[-2:]
    fields, chunk, _, lanes = next_ref.shape
    planes = now_ref.shape[1]
    step = pl.program_id(0)
    base = (first + step) * chunk
    span = range(fields)

    @pl.when(step == 0)
    def _():
        packed = y_halo([y_a_ref[f] for f in span], [y_b_ref[f] for f in span])
        for f in span:
            halo_ref[f] = packed[f]

    lines = pl.ds(pl.multiple_of(base, 8), chunk)
    x_lo, x_hi = sides("gx", [x_a_ref[f, lines, :] for f in span], [x_b_ref[f, lines, :] for f in span])
    x_behind = only_behind(x_lo, 1)
    x_ahead = only_ahead(x_hi, 1)
    turn = lax.rem(lanes - 2 * base, lanes)
    halo = [pltpu.roll(halo_ref[f], turn, 1) for f in span]
    z = jnp.maximum(base - 1, 0)
    before = only_behind([now_ref[f, z] for f in span], 3)
    pending = None

    def finish(j, ahead):
        for f in span:
            total = pending[f] + ahead[f]
            next_ref[f, j] = advanced(start_ref[f, base + j], now_ref[f, base + j], total)

    for j in range(chunk):
        q = [now_ref[f, base + j] for f in span]
        state = state_of(q)
        products = products_of(q, state)
        half = scaled(q)
        flux = flux_of(q, state, 3, products)
        if pending is not None:
            finish(j - 1, ahead_of(half, flux))
        edge = [pltpu.roll(halo[f], lanes - 1 - 2 * j, 1) for f in span]
        sums = within_plane(
            q, half, state, products, edge,
            [x_ahead[f][j : j + 1] for f in span], [x_behind[f][j : j + 1] for f in span],
        )
        pending = [sums[f] + before[f] for f in span]
        before = behind_of(half, flux)
    z = jnp.minimum(base + chunk, planes - 1)
    finish(chunk - 1, only_ahead([now_ref[f, z] for f in span], 3))


def stencil(now, start, around, first, count, into):
    fields, _, rows, lanes = now.shape
    chunk = CHUNK
    specs = [IN_VMEM] * 6
    operands = [now, start, *around]
    if into is not None:
        specs.append(pl.BlockSpec(memory_space=pl.ANY))
        operands.append(into)
    return pl.pallas_call(
        functools.partial(stencil_body, first),
        out_shape=jax.ShapeDtypeStruct(now.shape, now.dtype),
        grid=(count,),
        in_specs=specs,
        out_specs=pl.BlockSpec((fields, chunk, rows, lanes), lambda c: (0, first + c, 0, 0)),
        scratch_shapes=[pltpu.VMEM((fields, rows, lanes), jnp.float32)],
        input_output_aliases={} if into is None else {len(operands) - 1: 0},
        compiler_params=ROOM,
    )(*operands)


def relayout_body(older_ref, out_ref, *cells_refs):
    older, group, rows, lanes = older_ref.shape
    snaps = out_ref.shape[1]
    base = pl.program_id(0) * group
    stride = rows + 1

    @pl.when(pl.program_id(0) == 0)
    def _():
        for ref in cells_refs:
            for snap in range(older, snaps):
                ref[pl.ds(snap * stride, rows), :] = jnp.zeros((rows, lanes), jnp.float32)

    for which, ref in enumerate(cells_refs):
        for snap in range(older):
            ref[pl.ds(snap * stride, rows), :] = older_ref[snap, which].astype(jnp.float32)
    for which, ref in enumerate(cells_refs):
        for r in range(rows):
            part = ref[pl.ds(r, snaps, stride=stride), :]
            out_ref[base + which, :, r * lanes : (r + 1) * lanes] = part.astype(out_ref.dtype)


def relayout(history):
    older, samples, rows, lanes = history.shape
    snaps = older + 1
    group = 4
    return pl.pallas_call(
        relayout_body,
        out_shape=jax.ShapeDtypeStruct((samples, snaps, rows * lanes), history.dtype),
        grid=(samples // group,),
        in_specs=[pl.BlockSpec((older, group, rows, lanes), lambda p: (0, p, 0, 0))],
        out_specs=IN_VMEM,
        scratch_shapes=[pltpu.VMEM((snaps * (rows + 1), lanes), jnp.float32)] * group,
        compiler_params=ROOM,
        name="relayout",
    )(history)


def gram_body(
    cells_ref, now_ref, start_ref, y_a_ref, y_b_ref, x_a_ref, x_b_ref,
    mine_ref, sent_ref, newest_ref, total_ref, halo_ref, folded_ref, *, axis,
):
    snaps, width = cells_ref.shape[1:]
    pair = newest_ref.shape[0]
    fields, rows, lanes = halo_ref.shape
    step = pl.program_id(0)
    base = pair * jnp.maximum(step - 1, 0)
    groups = pl.num_programs(0) - 1
    span = range(fields)
    tile = 16

    @pl.when(step == 0)
    def _():
        newest_ref[...] = jnp.zeros_like(newest_ref)
        packed = y_halo([y_a_ref[f] for f in span], [y_b_ref[f] for f in span])
        for f in span:
            halo_ref[f] = packed[f]

    bottom = iota((tile, width), 0) == tile - 1
    parts = []
    for which in range(pair):
        row = jnp.concatenate([newest_ref[which, r : r + 1, :] for r in range(rows)], axis=1)
        last = cells_ref[base + which, snaps - tile :, :].astype(jnp.float32)
        last = jnp.where(bottom, row, last).astype(cells_ref.dtype)
        parts.append(jnp.concatenate([cells_ref[base + which, : snaps - tile, :], last], axis=0))
    matrix = jnp.concatenate(parts, axis=1)
    product = lax.dot_general(
        matrix, matrix, (((1,), (1,)), ((), ())), preferred_element_type=jnp.float32
    )

    def newest(which):
        z = ZSUB * (pair * jnp.minimum(step, groups - 1) + which)
        q = [now_ref[f, z] for f in span]
        state = state_of(q)
        products = products_of(q, state)
        half = scaled(q)
        turn = lax.rem(2 * lanes - 1 - 2 * z, lanes)
        edge = [pltpu.roll(halo_ref[f], turn, 1) for f in span]
        x_lo, x_hi = sides(
            "gx", [x_a_ref[f, pl.ds(z, 1), :] for f in span], [x_b_ref[f, pl.ds(z, 1), :] for f in span]
        )
        x_behind, x_ahead = only_behind(x_lo, 1), only_ahead(x_hi, 1)
        sums = within_plane(q, half, state, products, edge, x_ahead, x_behind)
        low = jnp.maximum(z - 1, 0)
        before = only_behind([now_ref[f, low] for f in span], 3)
        after = only_ahead([now_ref[f, z + 1] for f in span], 3)
        out = [advanced(start_ref[f, z], q[f], sums[f] + before[f] + after[f]) for f in span]
        return state_of(out)[1]

    fresh = [newest(which) for which in range(pair)]
    for which in range(pair):
        newest_ref[which] = fresh[which]
    total_ref[...] = jnp.where(step > 1, total_ref[...], 0.0) + product

    @pl.when(step == groups)
    def _():
        half = snaps // 2
        first, final = total_ref[:half, :half], total_ref[half:, half:]
        r, c = iota((half, half), 0), iota((half, half), 1)
        folded_ref[:half] = jnp.where(r <= c, first, final)
        folded_ref[half : 2 * half] = total_ref[:half, half:]
        diagonal = jnp.sum(jnp.where(r == c, final, 0.0), axis=0, keepdims=True)
        folded_ref[2 * half :] = jnp.broadcast_to(diagonal, (folded_ref.shape[0] - 2 * half, half))
        size = mine_ref.shape[0]
        side = lax.rem(lax.axis_index(axis), 2)
        mine_ref[...] = folded_ref[pl.ds(pl.multiple_of(side * size, 8), size), :]
        sent_ref[...] = folded_ref[pl.ds(pl.multiple_of((1 - side) * size, 8), size), :]


def gram(cells, now, start, around, axis):
    samples, snaps, _ = cells.shape
    fields, _, rows, lanes = now.shape
    half = snaps // 2
    pair = 2
    groups = samples // pair
    size = half + 8
    return pl.pallas_call(
        functools.partial(gram_body, axis=axis),
        out_shape=(jax.ShapeDtypeStruct((size, half), jnp.float32),) * 2,
        grid=(groups + 1,),
        in_specs=[IN_VMEM] * 7,
        out_specs=(IN_VMEM, IN_VMEM),
        scratch_shapes=[
            pltpu.VMEM((pair, rows, lanes), jnp.float32),
            pltpu.VMEM((snaps, snaps), jnp.float32),
            pltpu.VMEM((fields, rows, lanes), jnp.float32),
            pltpu.VMEM((2 * size, half), jnp.float32),
        ],
        compiler_params=ROOM,
        name="gram",
    )(cells, now, start, *around)


def factor_body(scale, axis, mine_ref, other_ref, out_ref, gram_ref, folded_ref):
    size, half = mine_ref.shape
    side = lax.rem(lax.axis_index(axis), 2)
    folded_ref[pl.ds(pl.multiple_of(side * size, 8), size), :] = mine_ref[...]
    folded_ref[pl.ds(pl.multiple_of((1 - side) * size, 8), size), :] = other_ref[...]
    group = 8
    r, c = iota((half, half), 0), iota((half, half), 1)
    mixed = folded_ref[:half] * scale
    turned = mixed.T
    gram_ref[:half, :half] = jnp.where(r <= c, mixed, turned)
    gram_ref[:half, half:] = folded_ref[half : 2 * half] * scale
    diagonal = jnp.broadcast_to(folded_ref[2 * half : 2 * half + 1] * scale, (half, half))
    gram_ref[half:, half:] = jnp.where(r == c, diagonal, jnp.where(r > c, mixed, turned))
    out_ref[half:, :half] = jnp.zeros((half, half), jnp.float32)
    sub, lane = iota((group, half), 0), iota((group, half), 1)
    span = range(group)

    def column(x, index):
        return jnp.broadcast_to(x[:, index : index + 1], (group, half))

    def line(x, index):
        return jnp.broadcast_to(x[index : index + 1, :], (group, half))

    per = half // group
    for panel in range(2):
        width = 2 - panel
        tiles = [
            [
                gram_ref[pl.ds(panel * half + group * t, group), pl.ds((panel + v) * half, half)]
                for v in range(width)
            ]
            for t in range(per)
        ]
        for t in range(per):
            first = group * t
            own = [column(tiles[t][0], first + j) for j in span]
            pivot = {(i, j): line(own[j], i) for j in span for i in range(j + 1)}
            rows = [[line(x, i) for x in tiles[t]] for i in span]
            later = range(t + 1, per)
            lower = {m: [column(tiles[m][0], first + j) for j in span] for m in later}
            for i in span:
                inverse = lax.rsqrt(pivot[i, i])
                for j in range(i + 1, group):
                    pivot[i, j] = pivot[i, j] * inverse
                for j in range(i + 1, group):
                    for k in range(j, group):
                        pivot[j, k] = pivot[j, k] - pivot[i, j] * pivot[i, k]
                rows[i] = [x * inverse for x in rows[i]]
                for j in range(i + 1, group):
                    rows[j] = [a - pivot[i, j] * b for a, b in zip(rows[j], rows[i])]
                for m in later:
                    entry = lower[m][i] * inverse
                    for j in range(i + 1, group):
                        lower[m][j] = lower[m][j] - entry * pivot[i, j]
                    tiles[m] = [a - entry * b for a, b in zip(tiles[m], rows[i])]
            for v in range(width):
                merged = rows[0][v]
                for i in range(1, group):
                    merged = jnp.where(sub == i, rows[i][v], merged)
                if v == 0:
                    merged = jnp.where(lane >= first + sub, merged, 0.0)
                out_ref[pl.ds(panel * half + first, group), pl.ds((panel + v) * half, half)] = merged
        if panel == 0:
            across = out_ref[:half, half:]
            gram_ref[half:, half:] = gram_ref[half:, half:] - lax.dot_general(
                across,
                across,
                (((0,), (0,)), ((), ())),
                precision=lax.Precision.HIGHEST,
                preferred_element_type=jnp.float32,
            )


def factor(mine, other, rows_total, axis):
    size, half = mine.shape
    return pl.pallas_call(
        functools.partial(factor_body, 1.0 / rows_total, axis),
        out_shape=jax.ShapeDtypeStruct((2 * half, 2 * half), jnp.float32),
        in_specs=[IN_VMEM, IN_VMEM],
        out_specs=IN_VMEM,
        scratch_shapes=[
            pltpu.VMEM((2 * half, 2 * half), jnp.float32),
            pltpu.VMEM((2 * size, half), jnp.float32),
        ],
        compiler_params=ROOM,
        name="factor",
    )(mine, other)


def rounds(count):
    groups = []
    bit = 2
    while bit < count:
        groups.append((bit, 2 * bit, 3 * bit) if 2 * bit < count else (bit,))
        bit *= 4
    return groups


def local(section_start, section_now, history):
    axes = ("gx", "gy")
    count = lax.axis_size("gx") * lax.axis_size("gy")
    first, second, cols = edges(pltpu.with_memory_space_constraint(section_now, pltpu.HBM))

    def neighbours(part, axis, by):
        size = lax.axis_size(axis)
        assert size % 2 == 0
        return lax.ppermute(part, axis, [(i, (i + by * (-1) ** i) % size) for i in range(size)])

    def swap(part, bit):
        return lax.ppermute(part, axes, [(i, i ^ bit) for i in range(count)])

    x_a, x_b = neighbours(first, "gx", 1), neighbours(second, "gx", -1)
    y_a, y_b = neighbours(cols, "gy", 1), neighbours(cols, "gy", -1)
    around = (y_a, y_b, x_a, x_b)
    cells = relayout(pltpu.with_memory_space_constraint(history, pltpu.HBM))
    mine, sent = gram(cells, section_now, section_start, around, "gy")
    part = mine + swap(sent, 1)
    for group in rounds(count):
        came = [swap(part, bits) for bits in group]
        part = part + came[0]
        if len(came) > 1:
            part = part + (came[1] + came[2])
    rows_total = history[0].size * count
    triangle = factor(part, swap(part, 1), rows_total, "gy")
    chunks = section_now.shape[1] // CHUNK
    section_next = None
    for piece in range(PIECES):
        low, high = piece * chunks // PIECES, (piece + 1) * chunks // PIECES
        section_next = stencil(section_now, section_start, around, low, high - low, section_next)
    return (section_next, triangle)


def solution(mesh):
    placed = P(None, None, "gx", "gy")
    return jax.shard_map(
        local,
        mesh=mesh,
        in_specs=(placed, placed, placed),
        out_specs=(placed, P()),
        check_vma=False,
    )
```
